32 devices in a mesh: groups: 2 (over y), seq: 16 (over z, x, core).
Axes of the slice: x: 2, y: 2, z: 4, core: 2. Of those that a mesh axis runs over, the one named last changes fastest.
Arguments:
- pool_kv: bfloat16 [3072, 1024], P(('groups', 'seq')), parts along dimension 0, may hold values from -6 to 6
- pool_slot: int32 [32], P('groups'), parts along dimension 0, may hold values from 0 to 15, each once
- passage_order: int32 [32], P('groups'), parts along dimension 0, may hold values from 0 to 15, each once
- passage_start: int32 [32], P('groups'), parts along dimension 0, may hold values from 0 to 6784, as said below
- recompute_pos: int32 [32, 56], P('groups'), parts along dimension 0, may hold values from 0 to 383, as said below
- page_table: int32 [3072], P('groups'), parts along dimension 0, may hold values from 0 to 1535, as said below
- fresh_q: bfloat16 [1792, 1024], P(('groups', 'seq')), parts along dimension 0, may hold values from -64 to 64
- fresh_kv: bfloat16 [1792, 256], P(('groups', 'seq')), parts along dimension 0, may hold values from -64 to 64
Outputs:
- attended: bfloat16 [1792, 1024], P(('groups', 'seq')), parts along dimension 0
- decode_cache: bfloat16 [3072, 1024], P(('groups', 'seq')), parts along dimension 0
The draws below stay inside these ranges and needn't reach their ends.
There are 2 independent parts, one for each index of `groups`. The reference program is written for one: setup_inputs(seed, part) draws one part's arguments, and reference() takes and returns one part's arrays. A program takes and returns all parts, laid end to end along the dimension named above; each array names one. Nothing has to cross between parts.
Inputs may be any that keep to these rules, and one draw needn't show every extreme that they name: `passage_start`: increases by at least 384 from one passage to the next; the first is 0 and the last is (15) * 384 + 1024. `recompute_pos`: each row holds 56 different positions of its passage in increasing order. `page_table`: every row of the decode cache receives exactly one page; of the 96 pages of one passage at most 6 go to the 96 rows of one owner, and that many do for some owner.
All inputs are finite; a program needn't handle non-finite values.
Results may differ from the reference program's by a relative error of at most 0.0075.
The reference program's roundings to bfloat16 on the way count: a program that leaves them out, or rounds other values in their place, can miss the bound.
Values may be sent and summed in bfloat16 or wider, within the bound.
A program may use at most 256 MiB of HBM per device.

```python
import jax
import jax.numpy as jnp
from jax import lax

HD = 128
GROUP = 8
TOK_DEV = 384
PAGE = 4
GAP = 1024
PASSAGES = 16
SEL = 56
P_DEV = 96
CONTEXT = 6144


def draw_passage_start(key, part):
    extra = jnp.sort(jax.random.randint(jax.random.fold_in(key, 3), (PASSAGES,), 0, GAP + 1))
    extra = extra.at[0].set(0).at[PASSAGES - 1].set(GAP)
    return (jnp.arange(PASSAGES, dtype=jnp.int32) * TOK_DEV + extra).astype(jnp.int32)


def draw_recompute_pos(key, part):
    row_keys = jax.random.split(jax.random.fold_in(key, 5), PASSAGES)

    def one_row(row_key):
        return jnp.sort(jax.random.permutation(row_key, TOK_DEV)[:SEL])
    return jax.vmap(one_row)(row_keys).astype(jnp.int32)


def draw_page_table(key, part):
    split_keys = jax.random.split(jax.random.fold_in(key, 9), 4)
    owner_map = jax.random.permutation(split_keys[0], PASSAGES)
    device_shift = jax.random.permutation(split_keys[1], PASSAGES)
    spread = max(PASSAGES, P_DEV)
    page_offset = jax.random.permutation(split_keys[2], spread)[:P_DEV] % PASSAGES
    slot_keys = jax.random.split(split_keys[3], PASSAGES)
    slot_order = jax.vmap(lambda slot_key: jax.random.permutation(slot_key, P_DEV))(slot_keys)
    owners = owner_map[(device_shift[:, None] + page_offset[None, :]) % PASSAGES]
    page_slots = slot_order[owners, jnp.arange(P_DEV)[None, :]]
    return (owners * P_DEV + page_slots).reshape(-1).astype(jnp.int32)


def fresh_parts(key):
    split_keys = jax.random.split(jax.random.fold_in(key, 11), 4)
    row_count = PASSAGES * SEL
    query_rows = jnp.clip(jax.random.normal(split_keys[1], (row_count, GROUP * HD)) * 3.0, -20.0, 20.0)
    key_rows = jnp.clip(jax.random.normal(split_keys[2], (row_count, HD)), -6.0, 6.0)
    value_rows = jnp.clip(jax.random.normal(split_keys[3], (row_count, HD)), -6.0, 6.0)
    return (query_rows, jnp.concatenate([key_rows, value_rows], axis=1))


def draw_fresh_q(key, part):
    return fresh_parts(key)[0].astype(jnp.bfloat16)


def draw_fresh_kv(key, part):
    return fresh_parts(key)[1].astype(jnp.bfloat16)


def shard_levels(rng, extent, cuts, smallest, top_value):
    gain, own = 1.0, jax.random.fold_in(rng, 6)
    for axis_at, parts in cuts:
        steps = jnp.exp(jax.random.uniform(jax.random.fold_in(own, axis_at), (parts,), jnp.float32, smallest / len(cuts), top_value / len(cuts)))
        gain = gain * jnp.repeat(steps, extent[axis_at] // parts).reshape([-1 if axis == axis_at else 1 for axis in range(len(extent))])
    return gain


def centred(stream_key, shape, scale, reach, cuts=(), kind=jnp.bfloat16):
    drawn = scale * jax.random.normal(stream_key, shape, jnp.float32)
    if cuts:
        drawn = drawn * shard_levels(stream_key, shape, cuts, -0.22, 0.18)
    return jnp.clip(drawn, -reach, reach).astype(kind)


def setup_inputs(seed: int = 0, part: int = 0) -> dict:
    keys = jax.random.split(jax.random.key(seed), 9)
    part_splits = jax.random.split(jax.random.fold_in(keys[8], part), 9)
    pool_kv = centred(part_splits[0], (PASSAGES * P_DEV, PAGE * 2 * HD), 1.0, 6.0, ((0, 16),))
    pool_slot = jax.random.permutation(part_splits[1], PASSAGES).astype(jnp.int32)
    passage_order = jax.random.permutation(part_splits[2], PASSAGES).astype(jnp.int32)
    passage_start = draw_passage_start(jax.random.fold_in(jax.random.fold_in(keys[8], part), 71), part)
    recompute_pos = draw_recompute_pos(jax.random.fold_in(jax.random.fold_in(keys[8], part), 71), part)
    page_table = draw_page_table(jax.random.fold_in(jax.random.fold_in(keys[8], part), 71), part)
    fresh_q = draw_fresh_q(jax.random.fold_in(jax.random.fold_in(keys[8], part), 71), part)
    fresh_kv = draw_fresh_kv(jax.random.fold_in(jax.random.fold_in(keys[8], part), 71), part)
    return {"pool_kv": pool_kv, "pool_slot": pool_slot, "passage_order": passage_order, "passage_start": passage_start, "recompute_pos": recompute_pos, "page_table": page_table, "fresh_q": fresh_q, "fresh_kv": fresh_kv}


ROPE_BASE = 500000.0


def rotate_pos(vector, positions):
    half_dim = vector.shape[-1] // 2
    frequency = ROPE_BASE ** (-(jnp.arange(half_dim, dtype=jnp.float32) * (2.0 / vector.shape[-1])))
    angles = positions.astype(jnp.float32)[..., None] * frequency
    cosine = jnp.cos(angles)
    sine = jnp.sin(angles)
    lower_half = vector[..., :half_dim]
    upper_half = vector[..., half_dim:]
    return jnp.concatenate([lower_half * cosine - upper_half * sine, upper_half * cosine + lower_half * sine], axis=-1)


def reference(pool_kv, pool_slot, passage_order, passage_start, recompute_pos, page_table, fresh_q, fresh_kv):
    page_ids = jnp.arange(P_DEV, dtype=jnp.int32)
    passage_ids = jnp.arange(PASSAGES, dtype=jnp.int32)
    spot_index = pool_slot[passage_order][:, None] * P_DEV + page_ids[None, :]
    pool_rows = (spot_index % PASSAGES) * P_DEV + spot_index // PASSAGES
    cached = pool_kv[pool_rows.reshape(-1)].reshape(PASSAGES, TOK_DEV, 2, HD)
    start_grid = jnp.broadcast_to(passage_start[:, None], (PASSAGES, TOK_DEV))
    shifted = rotate_pos(cached[:, :, 0, :].astype(jnp.float32), start_grid)
    fresh_rows = fresh_kv.reshape(PASSAGES, SEL, 2 * HD)
    fresh_pos = passage_start[:, None] + recompute_pos
    fresh_keys = rotate_pos(fresh_rows[:, :, :HD].astype(jnp.float32), fresh_pos)
    passage_grid = jnp.broadcast_to(passage_ids[:, None], (PASSAGES, SEL))
    key_rows = shifted.at[passage_grid, recompute_pos].set(fresh_keys).astype(jnp.bfloat16)
    value_rows = cached[:, :, 1, :].at[passage_grid, recompute_pos].set(fresh_rows[:, :, HD:])
    page_rows = jnp.stack([key_rows, value_rows], axis=2).reshape(PASSAGES * P_DEV, PAGE * 2 * HD)
    decode_cache = jnp.zeros_like(page_rows).at[page_table].set(page_rows)
    queries = rotate_pos(fresh_q.reshape(PASSAGES, SEL, GROUP, HD).astype(jnp.float32), fresh_pos[:, :, None]).astype(jnp.bfloat16)
    flat_keys = key_rows.reshape(CONTEXT, HD)
    flat_values = value_rows.reshape(CONTEXT, HD)
    key_index = jnp.arange(CONTEXT, dtype=jnp.int32)
    query_places = passage_ids[:, None] * TOK_DEV + recompute_pos

    def attend_passage(inputs):
        query_rows, query_place = inputs
        flat_queries = query_rows.reshape(SEL * GROUP, HD)
        limit = jnp.repeat(query_place, GROUP)
        scores = jnp.dot(flat_queries, flat_keys.T, preferred_element_type=jnp.float32) * (HD ** -0.5)
        allowed = key_index[None, :] <= limit[:, None]
        peak_score = jnp.max(jnp.where(allowed, scores, -jnp.inf), axis=1, keepdims=True)
        weights = jnp.where(allowed, jnp.exp(scores - peak_score), 0.0)
        weight_sum = jnp.sum(weights, axis=1, keepdims=True)
        mixed = jnp.dot(weights.astype(jnp.bfloat16), flat_values, preferred_element_type=jnp.float32) / weight_sum
        return mixed.astype(jnp.bfloat16).reshape(SEL, GROUP * HD)

    attended = lax.map(attend_passage, (queries, query_places)).reshape(PASSAGES * SEL, GROUP * HD)
    return attended, decode_cache
```

```python
import jax
import jax.numpy as jnp
from jax import lax
from jax.sharding import PartitionSpec as P

GROUP = 8
PAGE = 4


ROPE_BASE = 500000.0


def rotate_pos(vector, positions):
    half_dim = vector.shape[-1] // 2
    frequency = ROPE_BASE ** (-(jnp.arange(half_dim, dtype=jnp.float32) * (2.0 / vector.shape[-1])))
    angles = positions.astype(jnp.float32)[..., None] * frequency
    cosine = jnp.cos(angles)
    sine = jnp.sin(angles)
    lower_half = vector[..., :half_dim]
    upper_half = vector[..., half_dim:]
    return jnp.concatenate(
        [lower_half * cosine - upper_half * sine, upper_half * cosine + lower_half * sine], axis=-1
    )


def pick(one_hot, table):
    return jnp.dot(one_hot.astype(jnp.float32), table, precision=lax.Precision.HIGHEST)


def shards(
    pool_kv, pool_slot, passage_order, passage_start, recompute_pos, page_table, fresh_q, fresh_kv
):
    seq_count = lax.axis_size("seq")
    my_index = lax.axis_index("seq")
    page_count = pool_kv.shape[0]
    row_width = pool_kv.shape[1]
    head_dim = fresh_kv.shape[1] // 2
    half_dim = head_dim // 2
    sel_count = fresh_q.shape[0]
    tok_count = page_count * PAGE
    total_pages = seq_count * page_count
    total_toks = seq_count * tok_count
    total_sel = seq_count * sel_count
    bf16 = jnp.bfloat16

    pooled = lax.all_gather(
        pool_kv.reshape(tok_count, 2 * head_dim), "seq", axis=0, tiled=True
    )
    fresh = lax.all_gather(fresh_kv, "seq", axis=0, tiled=True)

    passage_ids = jnp.arange(seq_count, dtype=jnp.int32)
    placed = passage_order[:, None] == passage_ids[None, :]
    slots = jnp.sum(jnp.where(placed, pool_slot[None, :], 0), axis=1)

    frequency = ROPE_BASE ** (-(jnp.arange(half_dim, dtype=jnp.float32) * (2.0 / head_dim)))
    start_angles = passage_start.astype(jnp.float32)[:, None] * frequency
    start_table = jnp.concatenate([jnp.cos(start_angles), jnp.sin(start_angles)], axis=1)
    recompute_rows = recompute_pos.astype(jnp.float32)

    row_ids = jnp.arange(total_pages, dtype=jnp.int32)
    spot = (row_ids % page_count) * seq_count + row_ids // page_count
    row_slot = spot // page_count
    row_page = spot % page_count
    row_hot = row_slot[:, None] == slots[None, :]
    row_passage = jnp.sum(jnp.where(row_hot, passage_ids[None, :], 0), axis=1)
    row_turn = pick(row_hot, start_table)
    row_recompute = pick(row_hot, recompute_rows)
    lane = jnp.arange(PAGE, dtype=jnp.int32)
    row_tok = row_page[:, None] * PAGE + lane[None, :]
    replaced = jnp.any(
        row_recompute[:, None, :] == row_tok[:, :, None].astype(jnp.float32), axis=2
    )
    far = jnp.int32(2**30)
    cached_pos = jnp.where(replaced, far, row_passage[:, None] * tok_count + row_tok).reshape(-1)
    fresh_place = (passage_ids[:, None] * tok_count + recompute_pos).reshape(-1)
    key_pos = jnp.concatenate([cached_pos, fresh_place])

    raw = pooled[:, :head_dim].astype(jnp.float32).reshape(total_pages, PAGE, head_dim)
    cosine = row_turn[:, None, :half_dim]
    sine = row_turn[:, None, half_dim:]
    lower = raw[:, :, :half_dim]
    upper = raw[:, :, half_dim:]
    shifted = jnp.concatenate(
        [lower * cosine - upper * sine, upper * cosine + lower * sine], axis=-1
    ).astype(bf16)
    fresh_pos_all = (passage_start[:, None] + recompute_pos).reshape(-1)
    fresh_keys = rotate_pos(fresh[:, :head_dim].astype(jnp.float32), fresh_pos_all).astype(bf16)
    keys = jnp.concatenate([shifted.reshape(total_toks, head_dim), fresh_keys], axis=0)
    values = jnp.concatenate([pooled[:, head_dim:], fresh[:, head_dim:]], axis=0)

    my_rows = my_index * page_count + jnp.arange(page_count, dtype=jnp.int32)
    source = jnp.sum(
        jnp.where(
            page_table[None, :] == my_rows[:, None],
            jnp.arange(total_pages, dtype=jnp.int32)[None, :],
            0,
        ),
        axis=1,
    )
    source_passage = source // page_count
    source_page = source % page_count
    source_hot = source_passage[:, None] == passage_ids[None, :]
    source_spot = (
        jnp.sum(jnp.where(source_hot, slots[None, :], 0), axis=1) * page_count + source_page
    )
    source_row = (source_spot % seq_count) * page_count + source_spot // seq_count
    source_recompute = pick(source_hot, recompute_rows)
    source_tok = source_page[:, None] * PAGE + lane[None, :]
    match = source_recompute[:, None, :] == source_tok[:, :, None].astype(jnp.float32)
    sel_ids = jnp.arange(sel_count, dtype=jnp.int32)
    sel_at = jnp.sum(jnp.where(match, sel_ids[None, None, :] + 1, 0), axis=2)
    token_at = jnp.where(
        sel_at > 0,
        total_toks + source_passage[:, None] * sel_count + sel_at - 1,
        source_row[:, None] * PAGE + lane[None, :],
    ).reshape(-1)
    choose = (
        token_at[:, None] == jnp.arange(total_toks + total_sel, dtype=jnp.int32)[None, :]
    ).astype(bf16)
    page_keys = jnp.dot(choose, keys, preferred_element_type=jnp.float32).astype(bf16)
    page_values = jnp.dot(choose, values, preferred_element_type=jnp.float32).astype(bf16)
    decode_cache = jnp.concatenate([page_keys, page_values], axis=1).reshape(
        page_count, row_width
    )

    mine = (passage_ids == my_index)[:, None]
    picked = jnp.sum(jnp.where(mine, recompute_pos, 0), axis=0)
    start_pos = jnp.sum(jnp.where(mine[:, 0], passage_start, 0))
    queries = rotate_pos(
        fresh_q.reshape(sel_count, GROUP, head_dim).astype(jnp.float32),
        (start_pos + picked)[:, None],
    ).astype(bf16)
    query_rows = queries.reshape(-1, head_dim)
    query_pos = jnp.repeat(my_index * tok_count + picked, GROUP)
    attended = attend(query_rows, query_pos, keys, values, key_pos)
    return (attended.reshape(sel_count, GROUP * head_dim), decode_cache)


def attend(query_rows, query_pos, keys, values, key_pos):
    score_scale = keys.shape[1] ** (-0.5)
    scores = jnp.dot(query_rows, keys.T, preferred_element_type=jnp.float32) * score_scale
    allowed = key_pos[None, :] <= query_pos[:, None]
    peak = jnp.max(jnp.where(allowed, scores, -jnp.inf), axis=1)
    weights = jnp.where(allowed, jnp.exp(scores - peak[:, None]), 0.0)
    weight_sum = jnp.sum(weights, axis=1)
    weighted = jnp.dot(weights.astype(jnp.bfloat16), values, preferred_element_type=jnp.float32)
    return (weighted / weight_sum[:, None]).astype(jnp.bfloat16)


def solution(mesh):
    placed = (
        P(("groups", "seq"), None),
        P("groups"),
        P("groups"),
        P("groups"),
        P("groups", None),
        P("groups"),
        P(("groups", "seq"), None),
        P(("groups", "seq"), None),
    )
    return jax.shard_map(
        shards,
        mesh=mesh,
        in_specs=placed,
        out_specs=(P(("groups", "seq"), None), P(("groups", "seq"), None)),
        check_vma=False,
    )
```

```python
import jax
import jax.numpy as jnp
from jax import lax
from jax.experimental import pallas as pl
from jax.experimental.pallas import tpu as pltpu
from jax.sharding import PartitionSpec as P

GROUP = 8
PAGE = 4


ROPE_BASE = 500000.0


def rotate_pos(vector, positions):
    half_dim = vector.shape[-1] // 2
    frequency = ROPE_BASE ** (-(jnp.arange(half_dim, dtype=jnp.float32) * (2.0 / vector.shape[-1])))
    angles = positions.astype(jnp.float32)[..., None] * frequency
    cosine = jnp.cos(angles)
    sine = jnp.sin(angles)
    lower_half = vector[..., :half_dim]
    upper_half = vector[..., half_dim:]
    return jnp.concatenate(
        [lower_half * cosine - upper_half * sine, upper_half * cosine + lower_half * sine], axis=-1
    )


MESH = pl.DeviceIdType.MESH


def spread_kernel(count, block_ref, all_ref, send_sem, recv_sem, own_sem):
    rows = block_ref.shape[0]
    cut = rows * 3 // 5 // 16 * 16
    parts = (pl.ds(0, cut), pl.ds(cut, rows - cut))
    length = count // 4
    me = lax.axis_index("seq")
    at = me // 4
    inner = lax.rem(me, 4)
    core = lax.rem(inner, 2)
    across_inner = lax.rem(inner + 2, 4)
    across = at * 4 + across_inner
    sibling = me + 1 - 2 * core
    twin_inner = inner + 1 - 2 * core
    up, down = me + 4, me - 4
    has_up, has_down = at < length - 1, at > 0

    barrier = pltpu.get_barrier_semaphore()

    def greet(device):
        pl.semaphore_signal(barrier, inc=1, device_id={"seq": device}, device_id_type=MESH)

    greet(across)
    greet(sibling)
    pl.when(has_up)(lambda: greet(up))
    pl.when(has_down)(lambda: greet(down))
    pl.semaphore_wait(barrier, 2 + jnp.where(has_up, 1, 0) + jnp.where(has_down, 1, 0))

    def copy(part, block, way, device, own=False):
        source = block_ref.at[parts[part]] if own else all_ref.at[block, parts[part]]
        return pltpu.make_async_remote_copy(
            src_ref=source,
            dst_ref=all_ref.at[block, parts[part]],
            send_sem=send_sem.at[way, part, block],
            recv_sem=recv_sem.at[part, block],
            device_id={"seq": device},
            device_id_type=MESH,
        )

    def begin(part, block, way, device, own=False):
        copy(part, block, way, device, own).start()

    def arrive(part, block):
        copy(part, block, 0, sibling).wait_recv()

    local = pltpu.make_async_copy(block_ref, all_ref.at[me], own_sem)
    local.start()

    def send_own(act):
        act(1, me, 2, across, True)
        pl.when(has_up)(lambda: act(0, me, 0, up, True))
        pl.when(has_down)(lambda: act(0, me, 1, down, True))
        pl.when(has_up)(lambda: act(1, me, 0, up, True))
        pl.when(has_down)(lambda: act(1, me, 1, down, True))
        act(0, me, 2, across, True)
        act(1, me, 3, sibling, True)
        act(0, me, 3, sibling, True)

    def pass_across_first(act):
        pl.when(has_up)(lambda: act(1, across, 0, up))
        pl.when(has_down)(lambda: act(1, across, 1, down))
        act(1, across, 3, sibling)

    def each(step, act, wait):
        for way, exists, more, device, place in (
            (0, at - step >= 0, has_up, up, at - step),
            (1, at + step < length, has_down, down, at + step),
        ):
            for part, where, cross in ((0, inner, True), (1, inner, False), (1, across_inner, False)):
                block = place * 4 + where

                @pl.when(exists)
                def _(part=part, block=block, cross=cross, way=way, more=more, device=device):
                    if wait:
                        arrive(part, block)
                    pl.when(more)(lambda: act(part, block, way, device))
                    if cross:
                        act(part, block, 2, across)
                    act(part, block, 3, sibling)

    def crossed(step, act, wait):
        for exists, place in ((at - step >= 0, at - step), (at + step < length, at + step)):

            @pl.when(exists)
            def _(place=place):
                block = place * 4 + across_inner
                if wait:
                    arrive(0, block)
                act(0, block, 3, sibling)

    def crossed_here(act, wait):
        if wait:
            arrive(0, across)
        act(0, across, 3, sibling)

    send_own(begin)
    arrive(1, across)
    pass_across_first(begin)

    @pl.loop(1, length)
    def _(step):
        each(step, begin, True)

    crossed_here(begin, True)

    @pl.loop(1, length)
    def _(step):
        crossed(step, begin, True)

    @pl.loop(0, length)
    def _(place):
        for other in range(2):
            block = place * 4 + other * 2 + lax.rem(core + 1, 2)
            arrive(0, block)
            arrive(1, block)

    def settle(part, block, way, device, own=False):
        copy(part, block, way, device, own).wait_send()

    send_own(settle)
    pass_across_first(settle)

    @pl.loop(1, length)
    def _(step):
        each(step, settle, False)
        crossed(step, settle, False)

    crossed_here(settle, False)
    local.wait()


def spread(block, count):
    rows, width = block.shape
    return pl.pallas_call(
        lambda *refs: spread_kernel(count, *refs),
        out_shape=jax.ShapeDtypeStruct((count, rows, width), block.dtype),
        in_specs=[pl.BlockSpec(memory_space=pltpu.VMEM)],
        out_specs=pl.BlockSpec(memory_space=pl.ANY),
        scratch_shapes=[
            pltpu.SemaphoreType.DMA((4, 2, count)),
            pltpu.SemaphoreType.DMA((2, count)),
            pltpu.SemaphoreType.DMA,
        ],
        compiler_params=pltpu.CompilerParams(collective_id=0, has_side_effects=True),
    )(block)


def pick(one_hot, table):
    return jnp.dot(one_hot.astype(jnp.float32), table, precision=lax.Precision.HIGHEST)


def shards(
    pool_kv, pool_slot, passage_order, passage_start, recompute_pos, page_table, fresh_q, fresh_kv
):
    seq_count = lax.axis_size("seq")
    my_index = lax.axis_index("seq")
    page_count = pool_kv.shape[0]
    row_width = pool_kv.shape[1]
    head_dim = fresh_kv.shape[1] // 2
    half_dim = head_dim // 2
    sel_count = fresh_q.shape[0]
    tok_count = page_count * PAGE
    total_pages = seq_count * page_count
    bf16 = jnp.bfloat16

    unit = tok_count + sel_count
    block = jnp.concatenate([pool_kv.reshape(tok_count, 2 * head_dim), fresh_kv], axis=0)
    everything = spread(block, seq_count)

    passage_ids = jnp.arange(seq_count, dtype=jnp.int32)
    placed = passage_order[:, None] == passage_ids[None, :]
    slots = jnp.sum(jnp.where(placed, pool_slot[None, :], 0), axis=1)

    frequency = ROPE_BASE ** (-(jnp.arange(half_dim, dtype=jnp.float32) * (2.0 / head_dim)))
    start_angles = passage_start.astype(jnp.float32)[:, None] * frequency
    start_table = jnp.concatenate([jnp.cos(start_angles), jnp.sin(start_angles)], axis=1)
    recompute_rows = recompute_pos.astype(jnp.float32)

    row_ids = jnp.arange(total_pages, dtype=jnp.int32)
    spot = (row_ids % page_count) * seq_count + row_ids // page_count
    row_slot = spot // page_count
    row_page = spot % page_count
    row_hot = row_slot[:, None] == slots[None, :]
    row_passage = jnp.sum(jnp.where(row_hot, passage_ids[None, :], 0), axis=1)
    row_turn = pick(row_hot, start_table)
    row_recompute = pick(row_hot, recompute_rows)
    lane = jnp.arange(PAGE, dtype=jnp.int32)
    row_tok = row_page[:, None] * PAGE + lane[None, :]
    replaced = jnp.any(
        row_recompute[:, None, :] == row_tok[:, :, None].astype(jnp.float32), axis=2
    )
    far = jnp.int32(2**30)
    cached_pos = jnp.where(replaced, far, row_passage[:, None] * tok_count + row_tok).reshape(-1)
    fresh_place = passage_ids[:, None] * tok_count + recompute_pos
    key_pos = jnp.concatenate([cached_pos.reshape(seq_count, tok_count), fresh_place], axis=1)
    key_pos = key_pos.reshape(-1)

    fresh_angles = (passage_start[:, None] + recompute_pos).astype(jnp.float32)[
        :, :, None
    ] * frequency
    fresh_turn = jnp.concatenate([jnp.cos(fresh_angles), jnp.sin(fresh_angles)], axis=-1)
    cached_turn = jnp.broadcast_to(
        row_turn.reshape(seq_count, page_count, 1, head_dim),
        (seq_count, page_count, PAGE, head_dim),
    ).reshape(seq_count, tok_count, head_dim)
    turn = jnp.concatenate([cached_turn, fresh_turn], axis=1)
    raw = everything[:, :, :head_dim].astype(jnp.float32)
    cosine = turn[:, :, :half_dim]
    sine = turn[:, :, half_dim:]
    lower = raw[:, :, :half_dim]
    upper = raw[:, :, half_dim:]
    keys = (
        jnp.concatenate([lower * cosine - upper * sine, upper * cosine + lower * sine], axis=-1)
        .astype(bf16)
        .reshape(seq_count * unit, head_dim)
    )
    values = everything[:, :, head_dim:].reshape(seq_count * unit, head_dim)

    my_rows = my_index * page_count + jnp.arange(page_count, dtype=jnp.int32)
    source = jnp.sum(
        jnp.where(
            page_table[None, :] == my_rows[:, None],
            jnp.arange(total_pages, dtype=jnp.int32)[None, :],
            0,
        ),
        axis=1,
    )
    source_passage = source // page_count
    source_page = source % page_count
    source_hot = source_passage[:, None] == passage_ids[None, :]
    source_spot = (
        jnp.sum(jnp.where(source_hot, slots[None, :], 0), axis=1) * page_count + source_page
    )
    source_row = (source_spot % seq_count) * unit + source_spot // seq_count * PAGE
    source_recompute = pick(source_hot, recompute_rows)
    source_tok = source_page[:, None] * PAGE + lane[None, :]
    match = source_recompute[:, None, :] == source_tok[:, :, None].astype(jnp.float32)
    sel_ids = jnp.arange(sel_count, dtype=jnp.int32)
    sel_at = jnp.sum(jnp.where(match, sel_ids[None, None, :] + 1, 0), axis=2)
    token_at = jnp.where(
        sel_at > 0,
        source_passage[:, None] * unit + tok_count + sel_at - 1,
        source_row[:, None] + lane[None, :],
    ).reshape(-1)
    choose = (
        token_at[:, None] == jnp.arange(seq_count * unit, dtype=jnp.int32)[None, :]
    ).astype(bf16)
    page_keys = jnp.dot(choose, keys, preferred_element_type=jnp.float32).astype(bf16)
    page_values = jnp.dot(choose, values, preferred_element_type=jnp.float32).astype(bf16)
    decode_cache = jnp.concatenate([page_keys, page_values], axis=1).reshape(
        page_count, row_width
    )

    mine = (passage_ids == my_index)[:, None]
    picked = jnp.sum(jnp.where(mine, recompute_pos, 0), axis=0)
    start_pos = jnp.sum(jnp.where(mine[:, 0], passage_start, 0))
    queries = rotate_pos(
        fresh_q.reshape(sel_count, GROUP, head_dim).astype(jnp.float32),
        (start_pos + picked)[:, None],
    ).astype(bf16)
    query_rows = queries.reshape(-1, head_dim)
    query_pos = jnp.repeat(my_index * tok_count + picked, GROUP)
    attended = attend(query_rows, query_pos, keys, values, key_pos)
    return (attended.reshape(sel_count, GROUP * head_dim), decode_cache)


def attend(query_rows, query_pos, keys, values, key_pos):
    score_scale = keys.shape[1] ** (-0.5)
    scores = jnp.dot(query_rows, keys.T, preferred_element_type=jnp.float32) * score_scale
    allowed = key_pos[None, :] <= query_pos[:, None]
    peak = jnp.max(jnp.where(allowed, scores, -jnp.inf), axis=1)
    weights = jnp.where(allowed, jnp.exp(scores - peak[:, None]), 0.0)
    weight_sum = jnp.sum(weights, axis=1)
    weighted = jnp.dot(weights.astype(jnp.bfloat16), values, preferred_element_type=jnp.float32)
    return (weighted / weight_sum[:, None]).astype(jnp.bfloat16)


def solution(mesh):
    placed = (
        P(("groups", "seq"), None),
        P("groups"),
        P("groups"),
        P("groups"),
        P("groups", None),
        P("groups"),
        P(("groups", "seq"), None),
        P(("groups", "seq"), None),
    )
    return jax.shard_map(
        shards,
        mesh=mesh,
        in_specs=placed,
        out_specs=(P(("groups", "seq"), None), P(("groups", "seq"), None)),
        check_vma=False,
    )
```

```python
import jax
import jax.numpy as jnp
from jax import lax
from jax.experimental import pallas as pl
from jax.experimental.pallas import tpu as pltpu
from jax.sharding import PartitionSpec as P

GROUP = 8
PAGE = 4


ROPE_BASE = 500000.0


def rotate_pos(vector, positions):
    half_dim = vector.shape[-1] // 2
    frequency = ROPE_BASE ** (-(jnp.arange(half_dim, dtype=jnp.float32) * (2.0 / vector.shape[-1])))
    angles = positions.astype(jnp.float32)[..., None] * frequency
    cosine = jnp.cos(angles)
    sine = jnp.sin(angles)
    lower_half = vector[..., :half_dim]
    upper_half = vector[..., half_dim:]
    return jnp.concatenate(
        [lower_half * cosine - upper_half * sine, upper_half * cosine + lower_half * sine], axis=-1
    )


MESH = pl.DeviceIdType.MESH


def spread_kernel(count, block_ref, all_ref, send_sem, recv_sem, own_sem):
    rows = block_ref.shape[0]
    cut = rows * 3 // 5 // 16 * 16
    parts = (pl.ds(0, cut), pl.ds(cut, rows - cut))
    length = count // 4
    me = lax.axis_index("seq")
    at = me // 4
    inner = lax.rem(me, 4)
    core = lax.rem(inner, 2)
    across_inner = lax.rem(inner + 2, 4)
    across = at * 4 + across_inner
    sibling = me + 1 - 2 * core
    twin_inner = inner + 1 - 2 * core
    up, down = me + 4, me - 4
    has_up, has_down = at < length - 1, at > 0

    barrier = pltpu.get_barrier_semaphore()

    def greet(device):
        pl.semaphore_signal(barrier, inc=1, device_id={"seq": device}, device_id_type=MESH)

    greet(across)
    greet(sibling)
    pl.when(has_up)(lambda: greet(up))
    pl.when(has_down)(lambda: greet(down))
    pl.semaphore_wait(barrier, 2 + jnp.where(has_up, 1, 0) + jnp.where(has_down, 1, 0))

    def copy(part, block, way, device, own=False):
        source = block_ref.at[parts[part]] if own else all_ref.at[block, parts[part]]
        return pltpu.make_async_remote_copy(
            src_ref=source,
            dst_ref=all_ref.at[block, parts[part]],
            send_sem=send_sem.at[way, part, block],
            recv_sem=recv_sem.at[part, block],
            device_id={"seq": device},
            device_id_type=MESH,
        )

    def begin(part, block, way, device, own=False):
        copy(part, block, way, device, own).start()

    def arrive(part, block):
        copy(part, block, 0, sibling).wait_recv()

    local = pltpu.make_async_copy(block_ref, all_ref.at[me], own_sem)
    local.start()

    def send_own(act):
        act(1, me, 2, across, True)
        pl.when(has_up)(lambda: act(0, me, 0, up, True))
        pl.when(has_down)(lambda: act(0, me, 1, down, True))
        pl.when(has_up)(lambda: act(1, me, 0, up, True))
        pl.when(has_down)(lambda: act(1, me, 1, down, True))
        act(0, me, 2, across, True)
        act(1, me, 3, sibling, True)
        act(0, me, 3, sibling, True)

    def pass_across_first(act):
        pl.when(has_up)(lambda: act(1, across, 0, up))
        pl.when(has_down)(lambda: act(1, across, 1, down))
        act(1, across, 3, sibling)

    def each(step, act, wait):
        for way, exists, more, device, place in (
            (0, at - step >= 0, has_up, up, at - step),
            (1, at + step < length, has_down, down, at + step),
        ):
            for part, where, cross in ((0, inner, True), (1, inner, False), (1, across_inner, False)):
                block = place * 4 + where

                @pl.when(exists)
                def _(part=part, block=block, cross=cross, way=way, more=more, device=device):
                    if wait:
                        arrive(part, block)
                    pl.when(more)(lambda: act(part, block, way, device))
                    if cross:
                        act(part, block, 2, across)
                    act(part, block, 3, sibling)

    def crossed(step, act, wait):
        for exists, place in ((at - step >= 0, at - step), (at + step < length, at + step)):

            @pl.when(exists)
            def _(place=place):
                block = place * 4 + across_inner
                if wait:
                    arrive(0, block)
                act(0, block, 3, sibling)

    def crossed_here(act, wait):
        if wait:
            arrive(0, across)
        act(0, across, 3, sibling)

    send_own(begin)
    arrive(1, across)
    pass_across_first(begin)

    @pl.loop(1, length)
    def _(step):
        each(step, begin, True)

    crossed_here(begin, True)

    @pl.loop(1, length)
    def _(step):
        crossed(step, begin, True)

    @pl.loop(0, length)
    def _(place):
        for other in range(2):
            block = place * 4 + other * 2 + lax.rem(core + 1, 2)
            arrive(0, block)
            arrive(1, block)

    def settle(part, block, way, device, own=False):
        copy(part, block, way, device, own).wait_send()

    send_own(settle)
    pass_across_first(settle)

    @pl.loop(1, length)
    def _(step):
        each(step, settle, False)
        crossed(step, settle, False)

    crossed_here(settle, False)
    local.wait()


def spread(block, count):
    rows, width = block.shape
    return pl.pallas_call(
        lambda *refs: spread_kernel(count, *refs),
        out_shape=jax.ShapeDtypeStruct((count, rows, width), block.dtype),
        in_specs=[pl.BlockSpec(memory_space=pltpu.VMEM)],
        out_specs=pl.BlockSpec(memory_space=pl.ANY),
        scratch_shapes=[
            pltpu.SemaphoreType.DMA((4, 2, count)),
            pltpu.SemaphoreType.DMA((2, count)),
            pltpu.SemaphoreType.DMA,
        ],
        compiler_params=pltpu.CompilerParams(collective_id=0, has_side_effects=True),
    )(block)


def blend_kernel(
    all_ref, turn_ref, key_pos_ref, query_ref, query_pos_ref, token_ref,
    attended_ref, pages_ref, peak_ref, sum_ref, mixed_ref, page_ref,
):
    step = pl.program_id(0)
    together, unit, width = all_ref.shape
    head_dim = width // 2
    half_dim = head_dim // 2
    count = together * unit

    @pl.when(step == 0)
    def _():
        peak_ref[...] = jnp.full(peak_ref.shape, -1e30, jnp.float32)
        sum_ref[...] = jnp.zeros(sum_ref.shape, jnp.float32)
        mixed_ref[...] = jnp.zeros(mixed_ref.shape, jnp.float32)
        page_ref[...] = jnp.zeros(page_ref.shape, jnp.float32)

    rows = all_ref[...].reshape(count, width)
    raw = rows[:, :head_dim].astype(jnp.float32)
    values = rows[:, head_dim:]
    turn = turn_ref[...].reshape(count, head_dim)
    turned = pltpu.roll(turn, half_dim, 1)
    first = lax.broadcasted_iota(jnp.int32, (count, head_dim), 1) < half_dim
    cosine = jnp.where(first, turn, turned)
    sine = jnp.where(first, -turned, turn)
    keys = (raw * cosine + pltpu.roll(raw, half_dim, 1) * sine).astype(jnp.bfloat16)

    scores = lax.dot_general(
        query_ref[...], keys, (((1,), (1,)), ((), ())), preferred_element_type=jnp.float32
    ) * (head_dim ** (-0.5))
    scores = jnp.where(key_pos_ref[0] <= query_pos_ref[...], scores, -1e30)
    old_peak = peak_ref[...]
    peak = jnp.maximum(old_peak, jnp.max(scores, axis=1, keepdims=True))
    shrink = jnp.exp(old_peak - peak)
    weights = jnp.exp(scores - peak)
    peak_ref[...] = peak
    sum_ref[...] = sum_ref[...] * shrink + jnp.sum(weights, axis=1, keepdims=True)
    mixed_ref[...] = mixed_ref[...] * shrink + jnp.dot(
        weights.astype(jnp.bfloat16), values, preferred_element_type=jnp.float32
    )

    local = token_ref[...] - step * count
    lanes = lax.broadcasted_iota(jnp.int32, (token_ref.shape[0], count), 1)
    choose = jnp.where(lanes == local, 1.0, 0.0).astype(jnp.bfloat16)
    page_ref[:, :head_dim] += jnp.dot(choose, keys, preferred_element_type=jnp.float32)
    page_ref[:, head_dim:] += jnp.dot(choose, values, preferred_element_type=jnp.float32)

    @pl.when(step == pl.num_programs(0) - 1)
    def _():
        attended_ref[...] = (mixed_ref[...] / sum_ref[...]).astype(jnp.bfloat16)
        pages_ref[...] = page_ref[...].astype(jnp.bfloat16)


def blend(everything, turn, key_pos, queries, query_pos, tokens):
    count, unit, width = everything.shape
    head_dim = width // 2
    together = 4
    steps = count // together
    query_count = queries.shape[0]
    token_count = tokens.shape[0]

    def whole(shape):
        return pl.BlockSpec(shape, lambda i: (0, 0))

    return pl.pallas_call(
        blend_kernel,
        grid=(steps,),
        out_shape=(
            jax.ShapeDtypeStruct((query_count, head_dim), jnp.bfloat16),
            jax.ShapeDtypeStruct((token_count, width), jnp.bfloat16),
        ),
        in_specs=[
            pl.BlockSpec((together, unit, width), lambda i: (i, 0, 0)),
            pl.BlockSpec((together, unit, head_dim), lambda i: (i, 0, 0)),
            pl.BlockSpec((1, 1, together * unit), lambda i: (i, 0, 0)),
            whole((query_count, head_dim)),
            whole((query_count, 1)),
            whole((token_count, 1)),
        ],
        out_specs=(whole((query_count, head_dim)), whole((token_count, width))),
        scratch_shapes=[
            pltpu.VMEM((query_count, 1), jnp.float32),
            pltpu.VMEM((query_count, 1), jnp.float32),
            pltpu.VMEM((query_count, head_dim), jnp.float32),
            pltpu.VMEM((token_count, width), jnp.float32),
        ],
    )(
        everything,
        turn,
        key_pos.reshape(steps, 1, together * unit),
        queries,
        query_pos[:, None],
        tokens[:, None],
    )


def pick(one_hot, table):
    return jnp.dot(one_hot.astype(jnp.float32), table, precision=lax.Precision.HIGHEST)


def shards(
    pool_kv, pool_slot, passage_order, passage_start, recompute_pos, page_table, fresh_q, fresh_kv
):
    seq_count = lax.axis_size("seq")
    my_index = lax.axis_index("seq")
    page_count = pool_kv.shape[0]
    row_width = pool_kv.shape[1]
    head_dim = fresh_kv.shape[1] // 2
    half_dim = head_dim // 2
    sel_count = fresh_q.shape[0]
    tok_count = page_count * PAGE
    total_pages = seq_count * page_count
    bf16 = jnp.bfloat16

    filled = tok_count + sel_count
    unit = -(-filled // 64) * 64
    far = jnp.int32(2**30)

    passage_ids = jnp.arange(seq_count, dtype=jnp.int32)
    mine = (passage_ids == my_index)[:, None]
    picked = jnp.sum(jnp.where(mine, recompute_pos, 0), axis=0)
    start_pos = jnp.sum(jnp.where(mine[:, 0], passage_start, 0))
    fresh_pos = start_pos + picked
    fresh_keys = rotate_pos(fresh_kv[:, :head_dim].astype(jnp.float32), fresh_pos).astype(bf16)
    block = jnp.concatenate(
        [
            pool_kv.reshape(tok_count, 2 * head_dim),
            jnp.concatenate([fresh_keys, fresh_kv[:, head_dim:]], axis=1),
            jnp.zeros((unit - filled, 2 * head_dim), bf16),
        ],
        axis=0,
    )
    everything = spread(block, seq_count)

    placed = passage_order[:, None] == passage_ids[None, :]
    slots = jnp.sum(jnp.where(placed, pool_slot[None, :], 0), axis=1)

    frequency = ROPE_BASE ** (-(jnp.arange(half_dim, dtype=jnp.float32) * (2.0 / head_dim)))
    start_angles = passage_start.astype(jnp.float32)[:, None] * frequency
    start_table = jnp.concatenate([jnp.cos(start_angles), jnp.sin(start_angles)], axis=1)
    recompute_rows = recompute_pos.astype(jnp.float32)

    row_ids = jnp.arange(total_pages, dtype=jnp.int32)
    spot = (row_ids % page_count) * seq_count + row_ids // page_count
    row_slot = spot // page_count
    row_page = spot % page_count
    row_hot = row_slot[:, None] == slots[None, :]
    row_passage = jnp.sum(jnp.where(row_hot, passage_ids[None, :], 0), axis=1)
    row_turn = pick(row_hot, start_table)
    row_recompute = pick(row_hot, recompute_rows)
    lane = jnp.arange(PAGE, dtype=jnp.int32)
    row_tok = row_page[:, None] * PAGE + lane[None, :]
    replaced = jnp.any(
        row_recompute[:, None, :] == row_tok[:, :, None].astype(jnp.float32), axis=2
    )
    cached_pos = jnp.where(replaced, far, row_passage[:, None] * tok_count + row_tok).reshape(-1)
    fresh_place = passage_ids[:, None] * tok_count + recompute_pos
    key_pos = jnp.concatenate(
        [
            cached_pos.reshape(seq_count, tok_count),
            fresh_place,
            jnp.full((seq_count, unit - filled), far, jnp.int32),
        ],
        axis=1,
    )
    cached_turn = jnp.broadcast_to(
        row_turn.reshape(seq_count, page_count, 1, head_dim),
        (seq_count, page_count, PAGE, head_dim),
    ).reshape(seq_count, tok_count, head_dim)
    still = jnp.where(jnp.arange(head_dim) < half_dim, 1.0, 0.0).astype(jnp.float32)
    fresh_turn = jnp.broadcast_to(still, (seq_count, unit - tok_count, head_dim))
    turn = jnp.concatenate([cached_turn, fresh_turn], axis=1)

    my_rows = my_index * page_count + jnp.arange(page_count, dtype=jnp.int32)
    source = jnp.sum(
        jnp.where(
            page_table[None, :] == my_rows[:, None],
            jnp.arange(total_pages, dtype=jnp.int32)[None, :],
            0,
        ),
        axis=1,
    )
    source_passage = source // page_count
    source_page = source % page_count
    source_hot = source_passage[:, None] == passage_ids[None, :]
    source_spot = (
        jnp.sum(jnp.where(source_hot, slots[None, :], 0), axis=1) * page_count + source_page
    )
    source_row = (source_spot % seq_count) * unit + source_spot // seq_count * PAGE
    source_recompute = pick(source_hot, recompute_rows)
    source_tok = source_page[:, None] * PAGE + lane[None, :]
    match = source_recompute[:, None, :] == source_tok[:, :, None].astype(jnp.float32)
    sel_ids = jnp.arange(sel_count, dtype=jnp.int32)
    sel_at = jnp.sum(jnp.where(match, sel_ids[None, None, :] + 1, 0), axis=2)
    token_at = jnp.where(
        sel_at > 0,
        source_passage[:, None] * unit + tok_count + sel_at - 1,
        source_row[:, None] + lane[None, :],
    ).reshape(-1)
    queries = rotate_pos(
        fresh_q.reshape(sel_count, GROUP, head_dim).astype(jnp.float32), fresh_pos[:, None]
    ).astype(bf16)
    query_rows = queries.reshape(-1, head_dim)
    query_pos = jnp.repeat(my_index * tok_count + picked, GROUP)
    attended, pages = blend(everything, turn, key_pos, query_rows, query_pos, token_at)
    return (
        attended.reshape(sel_count, GROUP * head_dim),
        pages.reshape(page_count, row_width),
    )


def solution(mesh):
    placed = (
        P(("groups", "seq"), None),
        P("groups"),
        P("groups"),
        P("groups"),
        P("groups", None),
        P("groups"),
        P(("groups", "seq"), None),
        P(("groups", "seq"), None),
    )
    return jax.shard_map(
        shards,
        mesh=mesh,
        in_specs=placed,
        out_specs=(P(("groups", "seq"), None), P(("groups", "seq"), None)),
        check_vma=False,
    )
```

```python
import jax
import jax.numpy as jnp
from jax import lax
from jax.experimental import pallas as pl
from jax.experimental.pallas import tpu as pltpu
from jax.sharding import PartitionSpec as P

GROUP = 8
PAGE = 4


ROPE_BASE = 500000.0
LOG2_E = 1.4426950408889634


def rotate_pos(vector, positions):
    half_dim = vector.shape[-1] // 2
    frequency = ROPE_BASE ** (-(jnp.arange(half_dim, dtype=jnp.float32) * (2.0 / vector.shape[-1])))
    angles = positions.astype(jnp.float32)[..., None] * frequency
    cosine = jnp.cos(angles)
    sine = jnp.sin(angles)
    lower_half = vector[..., :half_dim]
    upper_half = vector[..., half_dim:]
    return jnp.concatenate(
        [lower_half * cosine - upper_half * sine, upper_half * cosine + lower_half * sine], axis=-1
    )


MESH = pl.DeviceIdType.MESH


def spread_kernel(count, block_ref, all_ref, send_sem, recv_sem, own_sem):
    rows = block_ref.shape[0]
    length = count // 4
    halves = max(2, 2 * (length - 1))
    cut = rows * (halves - 1) // halves // 16 * 16
    parts = (pl.ds(0, cut), pl.ds(cut, rows - cut))
    me = lax.axis_index("seq")
    at = me // 4
    inner = lax.rem(me, 4)
    core = lax.rem(inner, 2)
    across_inner = lax.rem(inner + 2, 4)
    across = at * 4 + across_inner
    sibling = me + 1 - 2 * core
    twin_inner = inner + 1 - 2 * core
    up, down = me + 4, me - 4
    has_up, has_down = at < length - 1, at > 0

    barrier = pltpu.get_barrier_semaphore()

    def greet(device):
        pl.semaphore_signal(barrier, inc=1, device_id={"seq": device}, device_id_type=MESH)

    greet(across)
    greet(sibling)
    pl.when(has_up)(lambda: greet(up))
    pl.when(has_down)(lambda: greet(down))
    pl.semaphore_wait(barrier, 2 + jnp.where(has_up, 1, 0) + jnp.where(has_down, 1, 0))

    def copy(part, block, way, device, own=False):
        source = block_ref.at[parts[part]] if own else all_ref.at[block, parts[part]]
        return pltpu.make_async_remote_copy(
            src_ref=source,
            dst_ref=all_ref.at[block, parts[part]],
            send_sem=send_sem.at[way, part, block],
            recv_sem=recv_sem.at[part, block],
            device_id={"seq": device},
            device_id_type=MESH,
        )

    def begin(part, block, way, device, own=False):
        copy(part, block, way, device, own).start()

    def arrive(part, block):
        copy(part, block, 0, sibling).wait_recv()

    local = pltpu.make_async_copy(block_ref, all_ref.at[me], own_sem)
    local.start()

    def send_own(act):
        act(1, me, 2, across, True)
        pl.when(has_up)(lambda: act(0, me, 0, up, True))
        pl.when(has_down)(lambda: act(0, me, 1, down, True))
        pl.when(has_up)(lambda: act(1, me, 0, up, True))
        pl.when(has_down)(lambda: act(1, me, 1, down, True))
        act(0, me, 2, across, True)
        act(1, me, 3, sibling, True)
        act(0, me, 3, sibling, True)

    def pass_across_first(act):
        pl.when(has_up)(lambda: act(1, across, 0, up))
        pl.when(has_down)(lambda: act(1, across, 1, down))
        act(1, across, 3, sibling)

    def each(step, act, wait):
        for part, where, cross in ((0, inner, True), (1, inner, False), (1, across_inner, False)):
            for way, exists, more, device, place in (
                (0, at - step >= 0, has_up, up, at - step),
                (1, at + step < length, has_down, down, at + step),
            ):
                block = place * 4 + where

                @pl.when(exists)
                def _(part=part, block=block, cross=cross, way=way, more=more, device=device):
                    if wait:
                        arrive(part, block)
                    pl.when(more)(lambda: act(part, block, way, device))
                    if cross:
                        act(part, block, 2, across)
                    act(part, block, 3, sibling)

    def crossed(step, act, wait):
        for exists, place in ((at - step >= 0, at - step), (at + step < length, at + step)):

            @pl.when(exists)
            def _(place=place):
                block = place * 4 + across_inner
                if wait:
                    arrive(0, block)
                act(0, block, 3, sibling)

    def crossed_here(act, wait):
        if wait:
            arrive(0, across)
        act(0, across, 3, sibling)

    send_own(begin)
    arrive(1, across)
    pass_across_first(begin)

    @pl.loop(1, length)
    def _(step):
        each(step, begin, True)
        pl.when(step == 1)(lambda: crossed_here(begin, True))
        pl.when(step > 1)(lambda: crossed(step - 1, begin, True))

    if length == 1:
        crossed_here(begin, True)
    else:
        crossed(length - 1, begin, True)

    @pl.loop(0, length)
    def _(place):
        for other in range(2):
            block = place * 4 + other * 2 + lax.rem(core + 1, 2)
            arrive(0, block)
            arrive(1, block)

    def settle(part, block, way, device, own=False):
        copy(part, block, way, device, own).wait_send()

    send_own(settle)
    pass_across_first(settle)

    @pl.loop(1, length)
    def _(step):
        each(step, settle, False)
        crossed(step, settle, False)

    crossed_here(settle, False)
    local.wait()


def spread(block, count):
    rows, width = block.shape
    return pl.pallas_call(
        lambda *refs: spread_kernel(count, *refs),
        out_shape=jax.ShapeDtypeStruct((count, rows, width), block.dtype),
        in_specs=[pl.BlockSpec(memory_space=pltpu.VMEM)],
        out_specs=pl.BlockSpec(memory_space=pl.ANY),
        scratch_shapes=[
            pltpu.SemaphoreType.DMA((4, 2, count)),
            pltpu.SemaphoreType.DMA((2, count)),
            pltpu.SemaphoreType.DMA,
        ],
        compiler_params=pltpu.CompilerParams(collective_id=0, has_side_effects=True),
    )(block)


def blend_kernel(
    all_ref, turn_ref, key_pos_ref, query_ref, query_pos_ref, token_ref,
    attended_ref, pages_ref, peak_ref, sum_ref, mixed_ref, page_key_ref, page_value_ref,
):
    step = pl.program_id(0)
    together, unit, width = all_ref.shape
    head_dim = width // 2
    half_dim = head_dim // 2
    count = together * unit

    @pl.when(step == 0)
    def _():
        peak_ref[...] = jnp.full(peak_ref.shape, -1e30, jnp.float32)
        sum_ref[...] = jnp.zeros(sum_ref.shape, jnp.float32)
        mixed_ref[...] = jnp.zeros(mixed_ref.shape, jnp.float32)
        page_key_ref[...] = jnp.zeros(page_key_ref.shape, jnp.float32)
        page_value_ref[...] = jnp.zeros(page_value_ref.shape, jnp.float32)

    rows = all_ref[...].reshape(count, width)
    raw = rows[:, :head_dim].astype(jnp.float32)
    values = rows[:, head_dim:]
    pages = turn_ref.shape[1]
    owner = lax.broadcasted_iota(jnp.int32, (unit, pages), 0) // PAGE
    expand = jnp.where(
        owner == lax.broadcasted_iota(jnp.int32, (unit, pages), 1), 1.0, 0.0
    ).astype(jnp.float32)
    at_row = lax.broadcasted_iota(jnp.int32, (unit, head_dim), 0)
    at_lane = lax.broadcasted_iota(jnp.int32, (unit, head_dim), 1)
    still = jnp.where((at_row >= pages * PAGE) & (at_lane < half_dim), 1.0, 0.0)
    turn = jnp.concatenate(
        [
            jnp.dot(
                expand,
                turn_ref[part],
                precision=lax.Precision.HIGHEST,
                preferred_element_type=jnp.float32,
            )
            + still
            for part in range(together)
        ],
        axis=0,
    )
    turned = pltpu.roll(turn, half_dim, 1)
    first = lax.broadcasted_iota(jnp.int32, (count, head_dim), 1) < half_dim
    cosine = jnp.where(first, turn, turned)
    sine = jnp.where(first, -turned, turn)
    keys = (raw * cosine + pltpu.roll(raw, half_dim, 1) * sine).astype(jnp.bfloat16)

    scores = lax.dot_general(
        query_ref[...], keys, (((1,), (1,)), ((), ())), preferred_element_type=jnp.float32
    )
    slope = head_dim ** (-0.5) * LOG2_E
    scores = jnp.where(key_pos_ref[0] <= query_pos_ref[...], scores, -1e30)
    old_peak = peak_ref[...]
    peak = jnp.maximum(old_peak, jnp.max(scores, axis=1, keepdims=True))
    shrink = jnp.exp2((old_peak - peak) * slope)
    weights = jnp.exp2((scores - peak) * slope)
    peak_ref[...] = peak
    sum_ref[...] = sum_ref[...] * shrink + jnp.sum(weights, axis=1, keepdims=True)
    mixed_ref[...] = mixed_ref[...] * shrink + jnp.dot(
        weights.astype(jnp.bfloat16), values, preferred_element_type=jnp.float32
    )

    local = token_ref[...] - step * count
    lanes = lax.broadcasted_iota(jnp.int32, (token_ref.shape[0], count), 1)
    choose = jnp.where(lanes == local, 1.0, 0.0).astype(jnp.bfloat16)
    page_key_ref[...] += jnp.dot(choose, keys, preferred_element_type=jnp.float32)
    page_value_ref[...] += jnp.dot(choose, values, preferred_element_type=jnp.float32)

    @pl.when(step == pl.num_programs(0) - 1)
    def _():
        mixed_ref[...] = mixed_ref[...] / sum_ref[...]
        for head in range(GROUP):
            attended_ref[:, head * head_dim : (head + 1) * head_dim] = mixed_ref[
                pl.ds(head, attended_ref.shape[0], stride=GROUP), :
            ].astype(jnp.bfloat16)
        for token in range(PAGE):
            for at, held in enumerate((page_key_ref, page_value_ref)):
                start = (2 * token + at) * head_dim
                pages_ref[:, start : start + head_dim] = held[
                    pl.ds(token, pages_ref.shape[0], stride=PAGE), :
                ].astype(jnp.bfloat16)


def blend(everything, turn, key_pos, queries, query_pos, tokens):
    count, unit, width = everything.shape
    head_dim = width // 2
    together = 4
    steps = count // together
    query_count = queries.shape[0]
    token_count = tokens.shape[0]

    def whole(shape):
        return pl.BlockSpec(shape, lambda i: (0, 0))

    return pl.pallas_call(
        blend_kernel,
        grid=(steps,),
        out_shape=(
            jax.ShapeDtypeStruct((query_count // GROUP, GROUP * head_dim), jnp.bfloat16),
            jax.ShapeDtypeStruct((token_count // PAGE, PAGE * width), jnp.bfloat16),
        ),
        in_specs=[
            pl.BlockSpec((together, unit, width), lambda i: (i, 0, 0)),
            pl.BlockSpec((together, token_count // PAGE, head_dim), lambda i: (i, 0, 0)),
            pl.BlockSpec((1, 1, together * unit), lambda i: (i, 0, 0)),
            whole((query_count, head_dim)),
            whole((query_count, 1)),
            whole((token_count, 1)),
        ],
        out_specs=(
            whole((query_count // GROUP, GROUP * head_dim)),
            whole((token_count // PAGE, PAGE * width)),
        ),
        scratch_shapes=[
            pltpu.VMEM((query_count, 1), jnp.float32),
            pltpu.VMEM((query_count, 1), jnp.float32),
            pltpu.VMEM((query_count, head_dim), jnp.float32),
            pltpu.VMEM((token_count, head_dim), jnp.float32),
            pltpu.VMEM((token_count, head_dim), jnp.float32),
        ],
    )(
        everything,
        turn,
        key_pos.reshape(steps, 1, together * unit),
        queries,
        query_pos[:, None],
        tokens[:, None],
    )


def pick(one_hot, table):
    return jnp.dot(one_hot.astype(jnp.float32), table, precision=lax.Precision.HIGHEST)


def shards(
    pool_kv, pool_slot, passage_order, passage_start, recompute_pos, page_table, fresh_q, fresh_kv
):
    seq_count = lax.axis_size("seq")
    my_index = lax.axis_index("seq")
    page_count = pool_kv.shape[0]
    head_dim = fresh_kv.shape[1] // 2
    half_dim = head_dim // 2
    sel_count = fresh_q.shape[0]
    tok_count = page_count * PAGE
    total_pages = seq_count * page_count
    bf16 = jnp.bfloat16

    filled = tok_count + sel_count
    unit = -(-filled // 64) * 64
    far = jnp.int32(2**30)

    passage_ids = jnp.arange(seq_count, dtype=jnp.int32)
    mine = (passage_ids == my_index)[:, None]
    picked = jnp.sum(jnp.where(mine, recompute_pos, 0), axis=0)
    start_pos = jnp.sum(jnp.where(mine[:, 0], passage_start, 0))
    fresh_pos = start_pos + picked
    fresh_keys = rotate_pos(fresh_kv[:, :head_dim].astype(jnp.float32), fresh_pos).astype(bf16)
    block = jnp.concatenate(
        [
            pool_kv.reshape(tok_count, 2 * head_dim),
            jnp.concatenate([fresh_keys, fresh_kv[:, head_dim:]], axis=1),
            jnp.zeros((unit - filled, 2 * head_dim), bf16),
        ],
        axis=0,
    )
    everything = spread(block, seq_count)

    placed = passage_order[:, None] == passage_ids[None, :]
    slots = jnp.sum(jnp.where(placed, pool_slot[None, :], 0), axis=1)

    frequency = ROPE_BASE ** (-(jnp.arange(half_dim, dtype=jnp.float32) * (2.0 / head_dim)))
    start_angles = passage_start.astype(jnp.float32)[:, None] * frequency
    start_table = jnp.concatenate([jnp.cos(start_angles), jnp.sin(start_angles)], axis=1)
    recompute_rows = recompute_pos.astype(jnp.float32)

    row_ids = jnp.arange(total_pages, dtype=jnp.int32)
    spot = (row_ids % page_count) * seq_count + row_ids // page_count
    row_slot = spot // page_count
    row_page = spot % page_count
    row_hot = row_slot[:, None] == slots[None, :]
    row_passage = jnp.sum(jnp.where(row_hot, passage_ids[None, :], 0), axis=1)
    row_turn = pick(row_hot, start_table)
    row_recompute = pick(row_hot, recompute_rows)
    lane = jnp.arange(PAGE, dtype=jnp.int32)
    row_tok = row_page[:, None] * PAGE + lane[None, :]
    replaced = jnp.any(
        row_recompute[:, None, :] == row_tok[:, :, None].astype(jnp.float32), axis=2
    )
    cached_pos = jnp.where(replaced, far, row_passage[:, None] * tok_count + row_tok).reshape(-1)
    fresh_place = passage_ids[:, None] * tok_count + recompute_pos
    key_pos = jnp.concatenate(
        [
            cached_pos.reshape(seq_count, tok_count),
            fresh_place,
            jnp.full((seq_count, unit - filled), far, jnp.int32),
        ],
        axis=1,
    )
    turn = row_turn.reshape(seq_count, page_count, head_dim)

    my_rows = my_index * page_count + jnp.arange(page_count, dtype=jnp.int32)
    source = jnp.sum(
        jnp.where(
            page_table[None, :] == my_rows[:, None],
            jnp.arange(total_pages, dtype=jnp.int32)[None, :],
            0,
        ),
        axis=1,
    )
    source_passage = source // page_count
    source_page = source % page_count
    source_hot = source_passage[:, None] == passage_ids[None, :]
    source_spot = (
        jnp.sum(jnp.where(source_hot, slots[None, :], 0), axis=1) * page_count + source_page
    )
    source_row = (source_spot % seq_count) * unit + source_spot // seq_count * PAGE
    source_recompute = pick(source_hot, recompute_rows)
    source_tok = source_page[:, None] * PAGE + lane[None, :]
    match = source_recompute[:, None, :] == source_tok[:, :, None].astype(jnp.float32)
    sel_ids = jnp.arange(sel_count, dtype=jnp.int32)
    sel_at = jnp.sum(jnp.where(match, sel_ids[None, None, :] + 1, 0), axis=2)
    token_at = jnp.where(
        sel_at > 0,
        source_passage[:, None] * unit + tok_count + sel_at - 1,
        source_row[:, None] + lane[None, :],
    ).reshape(-1)
    queries = rotate_pos(
        fresh_q.reshape(sel_count, GROUP, head_dim).astype(jnp.float32), fresh_pos[:, None]
    ).astype(bf16)
    query_rows = queries.reshape(-1, head_dim)
    query_pos = jnp.repeat(my_index * tok_count + picked, GROUP)
    attended, pages = blend(everything, turn, key_pos, query_rows, query_pos, token_at)
    return (attended, pages)


def solution(mesh):
    placed = (
        P(("groups", "seq"), None),
        P("groups"),
        P("groups"),
        P("groups"),
        P("groups", None),
        P("groups"),
        P(("groups", "seq"), None),
        P(("groups", "seq"), None),
    )
    return jax.shard_map(
        shards,
        mesh=mesh,
        in_specs=placed,
        out_specs=(P(("groups", "seq"), None), P(("groups", "seq"), None)),
        check_vma=False,
    )
```

```python
import jax
import jax.numpy as jnp
from jax import lax
from jax.experimental import pallas as pl
from jax.experimental.pallas import tpu as pltpu
from jax.sharding import PartitionSpec as P

GROUP = 8
PAGE = 4


ROPE_BASE = 500000.0
LOG2_E = 1.4426950408889634


def rotate_pos(vector, positions):
    half_dim = vector.shape[-1] // 2
    frequency = ROPE_BASE ** (-(jnp.arange(half_dim, dtype=jnp.float32) * (2.0 / vector.shape[-1])))
    angles = positions.astype(jnp.float32)[..., None] * frequency
    cosine = jnp.cos(angles)
    sine = jnp.sin(angles)
    lower_half = vector[..., :half_dim]
    upper_half = vector[..., half_dim:]
    return jnp.concatenate(
        [lower_half * cosine - upper_half * sine, upper_half * cosine + lower_half * sine], axis=-1
    )


MESH = pl.DeviceIdType.MESH


PIECES = 3


def piece_rows(rows, count):
    halves = max(2, 2 * (count // 4 - 1))
    cut = rows * (halves - 1) // halves // 16 * 16
    size = -(-cut // (PIECES * 16)) * 16
    return [(at, min(size, cut - at)) for at in range(0, cut, size)] + [(cut, rows - cut)]


def spread_kernel(count, block_ref, all_ref, send_sem, recv_sem, own_sem):
    rows = block_ref.shape[0]
    length = count // 4
    parts = [pl.ds(*piece) for piece in piece_rows(rows, count)]
    last = len(parts) - 1
    lined = range(last)
    me = lax.axis_index("seq")
    at = me // 4
    inner = lax.rem(me, 4)
    core = lax.rem(inner, 2)
    across_inner = lax.rem(inner + 2, 4)
    across = at * 4 + across_inner
    sibling = me + 1 - 2 * core
    twin_inner = inner + 1 - 2 * core
    up, down = me + 4, me - 4
    has_up, has_down = at < length - 1, at > 0

    barrier = pltpu.get_barrier_semaphore()

    def greet(device):
        pl.semaphore_signal(barrier, inc=1, device_id={"seq": device}, device_id_type=MESH)

    greet(across)
    greet(sibling)
    pl.when(has_up)(lambda: greet(up))
    pl.when(has_down)(lambda: greet(down))
    pl.semaphore_wait(barrier, 2 + jnp.where(has_up, 1, 0) + jnp.where(has_down, 1, 0))

    def copy(part, block, way, device, own=False):
        source = block_ref.at[parts[part]] if own else all_ref.at[block, parts[part]]
        return pltpu.make_async_remote_copy(
            src_ref=source,
            dst_ref=all_ref.at[block, parts[part]],
            send_sem=send_sem.at[way, part, block],
            recv_sem=recv_sem.at[part, block],
            device_id={"seq": device},
            device_id_type=MESH,
        )

    def begin(part, block, way, device, own=False):
        copy(part, block, way, device, own).start()

    def arrive(part, block):
        copy(part, block, 0, sibling).wait_recv()

    local = pltpu.make_async_copy(block_ref, all_ref.at[me], own_sem)
    local.start()

    def send_own(act):
        act(last, me, 2, across, True)
        for part in lined:
            pl.when(has_up)(lambda part=part: act(part, me, 0, up, True))
            pl.when(has_down)(lambda part=part: act(part, me, 1, down, True))
        pl.when(has_up)(lambda: act(last, me, 0, up, True))
        pl.when(has_down)(lambda: act(last, me, 1, down, True))
        for part in lined:
            act(part, me, 2, across, True)
        for part in (last, *lined):
            act(part, me, 3, sibling, True)

    def pass_across_first(act):
        pl.when(has_up)(lambda: act(last, across, 0, up))
        pl.when(has_down)(lambda: act(last, across, 1, down))
        act(last, across, 3, sibling)

    def each(step, act, wait):
        for part, where, cross in (
            *((part, inner, True) for part in lined),
            (last, inner, False),
            (last, across_inner, False),
        ):
            for way, exists, more, device, place in (
                (0, at - step >= 0, has_up, up, at - step),
                (1, at + step < length, has_down, down, at + step),
            ):
                block = place * 4 + where

                @pl.when(exists)
                def _(part=part, block=block, cross=cross, way=way, more=more, device=device):
                    if wait:
                        arrive(part, block)
                    pl.when(more)(lambda: act(part, block, way, device))
                    if cross:
                        act(part, block, 2, across)
                    act(part, block, 3, sibling)

    def crossed(step, act, wait):
        for exists, place in ((at - step >= 0, at - step), (at + step < length, at + step)):

            @pl.when(exists)
            def _(place=place):
                block = place * 4 + across_inner
                for part in lined:
                    if wait:
                        arrive(part, block)
                    act(part, block, 3, sibling)

    def crossed_here(act, wait):
        for part in lined:
            if wait:
                arrive(part, across)
            act(part, across, 3, sibling)

    send_own(begin)
    arrive(last, across)
    pass_across_first(begin)

    @pl.loop(1, length)
    def _(step):
        each(step, begin, True)
        pl.when(step == 1)(lambda: crossed_here(begin, True))
        pl.when(step > 1)(lambda: crossed(step - 1, begin, True))

    if length == 1:
        crossed_here(begin, True)
    else:
        crossed(length - 1, begin, True)

    @pl.loop(0, length)
    def _(place):
        for other in range(2):
            block = place * 4 + other * 2 + lax.rem(core + 1, 2)
            for part in range(last + 1):
                arrive(part, block)

    def settle(part, block, way, device, own=False):
        copy(part, block, way, device, own).wait_send()

    send_own(settle)
    pass_across_first(settle)

    @pl.loop(1, length)
    def _(step):
        each(step, settle, False)
        crossed(step, settle, False)

    crossed_here(settle, False)
    local.wait()


def spread(block, count):
    rows, width = block.shape
    return pl.pallas_call(
        lambda *refs: spread_kernel(count, *refs),
        out_shape=jax.ShapeDtypeStruct((count, rows, width), block.dtype),
        in_specs=[pl.BlockSpec(memory_space=pltpu.VMEM)],
        out_specs=pl.BlockSpec(memory_space=pl.ANY),
        scratch_shapes=[
            pltpu.SemaphoreType.DMA((4, len(piece_rows(rows, count)), count)),
            pltpu.SemaphoreType.DMA((len(piece_rows(rows, count)), count)),
            pltpu.SemaphoreType.DMA,
        ],
        compiler_params=pltpu.CompilerParams(collective_id=0, has_side_effects=True),
    )(block)


def blend_kernel(
    all_ref, turn_ref, key_pos_ref, query_ref, query_pos_ref, token_ref,
    attended_ref, pages_ref, peak_ref, sum_ref, mixed_ref, page_key_ref, page_value_ref,
):
    step = pl.program_id(0)
    together, unit, width = all_ref.shape
    head_dim = width // 2
    half_dim = head_dim // 2
    count = together * unit

    @pl.when(step == 0)
    def _():
        peak_ref[...] = jnp.full(peak_ref.shape, -1e30, jnp.float32)
        sum_ref[...] = jnp.zeros(sum_ref.shape, jnp.float32)
        mixed_ref[...] = jnp.zeros(mixed_ref.shape, jnp.float32)
        page_key_ref[...] = jnp.zeros(page_key_ref.shape, jnp.float32)
        page_value_ref[...] = jnp.zeros(page_value_ref.shape, jnp.float32)

    rows = all_ref[...].reshape(count, width)
    raw = rows[:, :head_dim].astype(jnp.float32)
    values = rows[:, head_dim:]
    pages = turn_ref.shape[1]
    owner = lax.broadcasted_iota(jnp.int32, (unit, pages), 0) // PAGE
    expand = jnp.where(
        owner == lax.broadcasted_iota(jnp.int32, (unit, pages), 1), 1.0, 0.0
    ).astype(jnp.float32)
    at_row = lax.broadcasted_iota(jnp.int32, (unit, head_dim), 0)
    at_lane = lax.broadcasted_iota(jnp.int32, (unit, head_dim), 1)
    still = jnp.where((at_row >= pages * PAGE) & (at_lane < half_dim), 1.0, 0.0)
    turn = jnp.concatenate(
        [
            jnp.dot(
                expand,
                turn_ref[part],
                precision=lax.Precision.HIGHEST,
                preferred_element_type=jnp.float32,
            )
            + still
            for part in range(together)
        ],
        axis=0,
    )
    turned = pltpu.roll(turn, half_dim, 1)
    first = lax.broadcasted_iota(jnp.int32, (count, head_dim), 1) < half_dim
    cosine = jnp.where(first, turn, turned)
    sine = jnp.where(first, -turned, turn)
    keys = (raw * cosine + pltpu.roll(raw, half_dim, 1) * sine).astype(jnp.bfloat16)

    scores = lax.dot_general(
        query_ref[...], keys, (((1,), (1,)), ((), ())), preferred_element_type=jnp.float32
    )
    slope = head_dim ** (-0.5) * LOG2_E
    scores = jnp.where(key_pos_ref[0] <= query_pos_ref[...], scores, -1e30)
    old_peak = peak_ref[...]
    peak = jnp.maximum(old_peak, jnp.max(scores, axis=1, keepdims=True))
    shrink = jnp.exp2((old_peak - peak) * slope)
    weights = jnp.exp2((scores - peak) * slope)
    peak_ref[...] = peak
    sum_ref[...] = sum_ref[...] * shrink + jnp.sum(weights, axis=1, keepdims=True)
    mixed_ref[...] = mixed_ref[...] * shrink + jnp.dot(
        weights.astype(jnp.bfloat16), values, preferred_element_type=jnp.float32
    )

    local = token_ref[...] - step * count
    lanes = lax.broadcasted_iota(jnp.int32, (token_ref.shape[0], count), 1)
    choose = jnp.where(lanes == local, 1.0, 0.0).astype(jnp.bfloat16)
    page_key_ref[...] += jnp.dot(choose, keys, preferred_element_type=jnp.float32)
    page_value_ref[...] += jnp.dot(choose, values, preferred_element_type=jnp.float32)

    @pl.when(step == pl.num_programs(0) - 1)
    def _():
        mixed_ref[...] = mixed_ref[...] / sum_ref[...]
        for head in range(GROUP):
            attended_ref[:, head * head_dim : (head + 1) * head_dim] = mixed_ref[
                pl.ds(head, attended_ref.shape[0], stride=GROUP), :
            ].astype(jnp.bfloat16)
        for token in range(PAGE):
            for at, held in enumerate((page_key_ref, page_value_ref)):
                start = (2 * token + at) * head_dim
                pages_ref[:, start : start + head_dim] = held[
                    pl.ds(token, pages_ref.shape[0], stride=PAGE), :
                ].astype(jnp.bfloat16)


def blend(everything, turn, key_pos, queries, query_pos, tokens):
    count, unit, width = everything.shape
    head_dim = width // 2
    together = 4
    steps = count // together
    query_count = queries.shape[0]
    token_count = tokens.shape[0]

    def whole(shape):
        return pl.BlockSpec(shape, lambda i: (0, 0))

    return pl.pallas_call(
        blend_kernel,
        grid=(steps,),
        out_shape=(
            jax.ShapeDtypeStruct((query_count // GROUP, GROUP * head_dim), jnp.bfloat16),
            jax.ShapeDtypeStruct((token_count // PAGE, PAGE * width), jnp.bfloat16),
        ),
        in_specs=[
            pl.BlockSpec((together, unit, width), lambda i: (i, 0, 0)),
            pl.BlockSpec((together, token_count // PAGE, head_dim), lambda i: (i, 0, 0)),
            pl.BlockSpec((1, 1, together * unit), lambda i: (i, 0, 0)),
            whole((query_count, head_dim)),
            whole((query_count, 1)),
            whole((token_count, 1)),
        ],
        out_specs=(
            whole((query_count // GROUP, GROUP * head_dim)),
            whole((token_count // PAGE, PAGE * width)),
        ),
        scratch_shapes=[
            pltpu.VMEM((query_count, 1), jnp.float32),
            pltpu.VMEM((query_count, 1), jnp.float32),
            pltpu.VMEM((query_count, head_dim), jnp.float32),
            pltpu.VMEM((token_count, head_dim), jnp.float32),
            pltpu.VMEM((token_count, head_dim), jnp.float32),
        ],
    )(
        everything,
        turn,
        key_pos.reshape(steps, 1, together * unit),
        queries,
        query_pos[:, None],
        tokens[:, None],
    )


def pick(one_hot, table):
    return jnp.dot(one_hot.astype(jnp.float32), table, precision=lax.Precision.HIGHEST)


def shards(
    pool_kv, pool_slot, passage_order, passage_start, recompute_pos, page_table, fresh_q, fresh_kv
):
    seq_count = lax.axis_size("seq")
    my_index = lax.axis_index("seq")
    page_count = pool_kv.shape[0]
    head_dim = fresh_kv.shape[1] // 2
    half_dim = head_dim // 2
    sel_count = fresh_q.shape[0]
    tok_count = page_count * PAGE
    total_pages = seq_count * page_count
    bf16 = jnp.bfloat16

    filled = tok_count + sel_count
    unit = -(-filled // 64) * 64
    far = jnp.int32(2**30)

    passage_ids = jnp.arange(seq_count, dtype=jnp.int32)
    mine = (passage_ids == my_index)[:, None]
    picked = jnp.sum(jnp.where(mine, recompute_pos, 0), axis=0)
    start_pos = jnp.sum(jnp.where(mine[:, 0], passage_start, 0))
    fresh_pos = start_pos + picked
    fresh_keys = rotate_pos(fresh_kv[:, :head_dim].astype(jnp.float32), fresh_pos).astype(bf16)
    block = jnp.concatenate(
        [
            pool_kv.reshape(tok_count, 2 * head_dim),
            jnp.concatenate([fresh_keys, fresh_kv[:, head_dim:]], axis=1),
            jnp.zeros((unit - filled, 2 * head_dim), bf16),
        ],
        axis=0,
    )
    everything = spread(block, seq_count)

    placed = passage_order[:, None] == passage_ids[None, :]
    slots = jnp.sum(jnp.where(placed, pool_slot[None, :], 0), axis=1)

    frequency = ROPE_BASE ** (-(jnp.arange(half_dim, dtype=jnp.float32) * (2.0 / head_dim)))
    start_angles = passage_start.astype(jnp.float32)[:, None] * frequency
    start_table = jnp.concatenate([jnp.cos(start_angles), jnp.sin(start_angles)], axis=1)
    recompute_rows = recompute_pos.astype(jnp.float32)

    row_ids = jnp.arange(total_pages, dtype=jnp.int32)
    spot = (row_ids % page_count) * seq_count + row_ids // page_count
    row_slot = spot // page_count
    row_page = spot % page_count
    row_hot = row_slot[:, None] == slots[None, :]
    row_passage = jnp.sum(jnp.where(row_hot, passage_ids[None, :], 0), axis=1)
    row_turn = pick(row_hot, start_table)
    row_recompute = pick(row_hot, recompute_rows)
    lane = jnp.arange(PAGE, dtype=jnp.int32)
    row_tok = row_page[:, None] * PAGE + lane[None, :]
    replaced = jnp.any(
        row_recompute[:, None, :] == row_tok[:, :, None].astype(jnp.float32), axis=2
    )
    cached_pos = jnp.where(replaced, far, row_passage[:, None] * tok_count + row_tok).reshape(-1)
    fresh_place = passage_ids[:, None] * tok_count + recompute_pos
    key_pos = jnp.concatenate(
        [
            cached_pos.reshape(seq_count, tok_count),
            fresh_place,
            jnp.full((seq_count, unit - filled), far, jnp.int32),
        ],
        axis=1,
    )
    turn = row_turn.reshape(seq_count, page_count, head_dim)

    my_rows = my_index * page_count + jnp.arange(page_count, dtype=jnp.int32)
    source = jnp.sum(
        jnp.where(
            page_table[None, :] == my_rows[:, None],
            jnp.arange(total_pages, dtype=jnp.int32)[None, :],
            0,
        ),
        axis=1,
    )
    source_passage = source // page_count
    source_page = source % page_count
    source_hot = source_passage[:, None] == passage_ids[None, :]
    source_spot = (
        jnp.sum(jnp.where(source_hot, slots[None, :], 0), axis=1) * page_count + source_page
    )
    source_row = (source_spot % seq_count) * unit + source_spot // seq_count * PAGE
    source_recompute = pick(source_hot, recompute_rows)
    source_tok = source_page[:, None] * PAGE + lane[None, :]
    match = source_recompute[:, None, :] == source_tok[:, :, None].astype(jnp.float32)
    sel_ids = jnp.arange(sel_count, dtype=jnp.int32)
    sel_at = jnp.sum(jnp.where(match, sel_ids[None, None, :] + 1, 0), axis=2)
    token_at = jnp.where(
        sel_at > 0,
        source_passage[:, None] * unit + tok_count + sel_at - 1,
        source_row[:, None] + lane[None, :],
    ).reshape(-1)
    queries = rotate_pos(
        fresh_q.reshape(sel_count, GROUP, head_dim).astype(jnp.float32), fresh_pos[:, None]
    ).astype(bf16)
    query_rows = queries.reshape(-1, head_dim)
    query_pos = jnp.repeat(my_index * tok_count + picked, GROUP)
    attended, pages = blend(everything, turn, key_pos, query_rows, query_pos, token_at)
    return (attended, pages)


def solution(mesh):
    placed = (
        P(("groups", "seq"), None),
        P("groups"),
        P("groups"),
        P("groups"),
        P("groups", None),
        P("groups"),
        P(("groups", "seq"), None),
        P(("groups", "seq"), None),
    )
    return jax.shard_map(
        shards,
        mesh=mesh,
        in_specs=placed,
        out_specs=(P(("groups", "seq"), None), P(("groups", "seq"), None)),
        check_vma=False,
    )
```

```python
import jax
import jax.numpy as jnp
from jax import lax
from jax.experimental import pallas as pl
from jax.experimental.pallas import tpu as pltpu
from jax.sharding import PartitionSpec as P

GROUP = 8
PAGE = 4


ROPE_BASE = 500000.0
LOG2_E = 1.4426950408889634


def rotate_pos(vector, positions):
    half_dim = vector.shape[-1] // 2
    frequency = ROPE_BASE ** (-(jnp.arange(half_dim, dtype=jnp.float32) * (2.0 / vector.shape[-1])))
    angles = positions.astype(jnp.float32)[..., None] * frequency
    cosine = jnp.cos(angles)
    sine = jnp.sin(angles)
    lower_half = vector[..., :half_dim]
    upper_half = vector[..., half_dim:]
    return jnp.concatenate(
        [lower_half * cosine - upper_half * sine, upper_half * cosine + lower_half * sine], axis=-1
    )


MESH = pl.DeviceIdType.MESH


PIECES = 3


def piece_rows(rows, count):
    halves = max(2, 2 * (count // 4 - 1))
    cut = rows * (halves - 1) // halves // 16 * 16
    size = -(-cut // (PIECES * 16)) * 16
    return [(at, min(size, cut - at)) for at in range(0, cut, size)] + [(cut, rows - cut)]


def spread_kernel(count, block_ref, all_ref, send_sem, recv_sem, own_sem):
    rows = block_ref.shape[0]
    length = count // 4
    parts = [pl.ds(*piece) for piece in piece_rows(rows, count)]
    last = len(parts) - 1
    lined = range(last)
    me = lax.axis_index("seq")
    at = me // 4
    inner = lax.rem(me, 4)
    core = lax.rem(inner, 2)
    across_inner = lax.rem(inner + 2, 4)
    across = at * 4 + across_inner
    sibling = me + 1 - 2 * core
    twin_inner = inner + 1 - 2 * core
    up, down = me + 4, me - 4
    has_up, has_down = at < length - 1, at > 0

    barrier = pltpu.get_barrier_semaphore()

    def greet(device):
        pl.semaphore_signal(barrier, inc=1, device_id={"seq": device}, device_id_type=MESH)

    greet(across)
    greet(sibling)
    pl.when(has_up)(lambda: greet(up))
    pl.when(has_down)(lambda: greet(down))
    pl.semaphore_wait(barrier, 2 + jnp.where(has_up, 1, 0) + jnp.where(has_down, 1, 0))

    def copy(part, block, way, device, own=False):
        source = block_ref.at[parts[part]] if own else all_ref.at[block, parts[part]]
        return pltpu.make_async_remote_copy(
            src_ref=source,
            dst_ref=all_ref.at[block, parts[part]],
            send_sem=send_sem.at[way, part, block],
            recv_sem=recv_sem.at[part, block],
            device_id={"seq": device},
            device_id_type=MESH,
        )

    def begin(part, block, way, device, own=False):
        copy(part, block, way, device, own).start()

    def arrive(part, block):
        copy(part, block, 0, sibling).wait_recv()

    local = pltpu.make_async_copy(block_ref, all_ref.at[me], own_sem)
    local.start()

    def send_own(act):
        act(last, me, 2, across, True)
        for part in lined:
            pl.when(has_up)(lambda part=part: act(part, me, 0, up, True))
            pl.when(has_down)(lambda part=part: act(part, me, 1, down, True))
        pl.when(has_up)(lambda: act(last, me, 0, up, True))
        pl.when(has_down)(lambda: act(last, me, 1, down, True))
        for part in lined:
            act(part, me, 2, across, True)
        for part in (last, *lined):
            act(part, me, 3, sibling, True)

    def pass_across_first(act):
        pl.when(has_up)(lambda: act(last, across, 0, up))
        pl.when(has_down)(lambda: act(last, across, 1, down))
        act(last, across, 3, sibling)

    def each(step, act, wait):
        for part, where, cross in (
            *((part, inner, True) for part in lined),
            (last, inner, False),
            (last, across_inner, False),
        ):
            for way, exists, more, device, place in (
                (0, at - step >= 0, has_up, up, at - step),
                (1, at + step < length, has_down, down, at + step),
            ):
                block = place * 4 + where

                @pl.when(exists)
                def _(part=part, block=block, cross=cross, way=way, more=more, device=device):
                    if wait:
                        arrive(part, block)
                    pl.when(more)(lambda: act(part, block, way, device))
                    if cross:
                        act(part, block, 2, across)
                    act(part, block, 3, sibling)

    def crossed(step, act, wait):
        for exists, place in ((at - step >= 0, at - step), (at + step < length, at + step)):

            @pl.when(exists)
            def _(place=place):
                block = place * 4 + across_inner
                for part in lined:
                    if wait:
                        arrive(part, block)
                    act(part, block, 3, sibling)

    def crossed_here(act, wait):
        for part in lined:
            if wait:
                arrive(part, across)
            act(part, across, 3, sibling)

    send_own(begin)
    arrive(last, across)
    pass_across_first(begin)

    @pl.loop(1, length)
    def _(step):
        each(step, begin, True)
        pl.when(step == 1)(lambda: crossed_here(begin, True))
        pl.when(step > 1)(lambda: crossed(step - 1, begin, True))

    if length == 1:
        crossed_here(begin, True)
    else:
        crossed(length - 1, begin, True)

    @pl.loop(0, length)
    def _(place):
        for other in range(2):
            block = place * 4 + other * 2 + lax.rem(core + 1, 2)
            for part in range(last + 1):
                arrive(part, block)

    def settle(part, block, way, device, own=False):
        copy(part, block, way, device, own).wait_send()

    send_own(settle)
    pass_across_first(settle)

    @pl.loop(1, length)
    def _(step):
        each(step, settle, False)
        crossed(step, settle, False)

    crossed_here(settle, False)
    local.wait()


def spread(block, count):
    rows, width = block.shape
    return pl.pallas_call(
        lambda *refs: spread_kernel(count, *refs),
        out_shape=jax.ShapeDtypeStruct((count, rows, width), block.dtype),
        in_specs=[pl.BlockSpec(memory_space=pltpu.VMEM)],
        out_specs=pl.BlockSpec(memory_space=pltpu.VMEM),
        scratch_shapes=[
            pltpu.SemaphoreType.DMA((4, len(piece_rows(rows, count)), count)),
            pltpu.SemaphoreType.DMA((len(piece_rows(rows, count)), count)),
            pltpu.SemaphoreType.DMA,
        ],
        compiler_params=pltpu.CompilerParams(collective_id=0, has_side_effects=True),
    )(block)


def blend_kernel(
    all_ref, turn_ref, key_pos_ref, query_ref, query_pos_ref, token_ref,
    attended_ref, pages_ref, peak_ref, sum_ref, mixed_ref, page_key_ref, page_value_ref,
):
    step = pl.program_id(0)
    together, unit, width = all_ref.shape
    head_dim = width // 2
    half_dim = head_dim // 2
    count = together * unit

    @pl.when(step == 0)
    def _():
        peak_ref[...] = jnp.full(peak_ref.shape, -1e30, jnp.float32)
        sum_ref[...] = jnp.zeros(sum_ref.shape, jnp.float32)
        mixed_ref[...] = jnp.zeros(mixed_ref.shape, jnp.float32)
        page_key_ref[...] = jnp.zeros(page_key_ref.shape, jnp.float32)
        page_value_ref[...] = jnp.zeros(page_value_ref.shape, jnp.float32)

    rows = all_ref[...].reshape(count, width)
    raw = rows[:, :head_dim].astype(jnp.float32)
    values = rows[:, head_dim:]
    pages = turn_ref.shape[1]
    owner = lax.broadcasted_iota(jnp.int32, (unit, pages), 0) // PAGE
    expand = jnp.where(
        owner == lax.broadcasted_iota(jnp.int32, (unit, pages), 1), 1.0, 0.0
    ).astype(jnp.bfloat16)

    def unfold(table):
        high = table.astype(jnp.bfloat16)
        rest = table - high.astype(jnp.float32)
        middle = rest.astype(jnp.bfloat16)
        low = (rest - middle.astype(jnp.float32)).astype(jnp.bfloat16)
        thirds = jnp.dot(
            expand,
            jnp.concatenate([high, middle, low], axis=1),
            preferred_element_type=jnp.float32,
        )
        return (
            thirds[:, :head_dim]
            + thirds[:, head_dim : 2 * head_dim]
            + thirds[:, 2 * head_dim :]
        )

    at_row = lax.broadcasted_iota(jnp.int32, (unit, head_dim), 0)
    at_lane = lax.broadcasted_iota(jnp.int32, (unit, head_dim), 1)
    still = jnp.where((at_row >= pages * PAGE) & (at_lane < half_dim), 1.0, 0.0)
    turn = jnp.concatenate(
        [
            unfold(turn_ref[part])
            + still
            for part in range(together)
        ],
        axis=0,
    )
    turned = pltpu.roll(turn, half_dim, 1)
    first = lax.broadcasted_iota(jnp.int32, (count, head_dim), 1) < half_dim
    cosine = jnp.where(first, turn, turned)
    sine = jnp.where(first, -turned, turn)
    keys = (raw * cosine + pltpu.roll(raw, half_dim, 1) * sine).astype(jnp.bfloat16)

    scores = lax.dot_general(
        query_ref[...], keys, (((1,), (1,)), ((), ())), preferred_element_type=jnp.float32
    )
    slope = head_dim ** (-0.5) * LOG2_E
    scores = jnp.where(key_pos_ref[0] <= query_pos_ref[...], scores, -1e30)
    old_peak = peak_ref[...]
    peak = jnp.maximum(old_peak, jnp.max(scores, axis=1, keepdims=True))
    shrink = jnp.exp2((old_peak - peak) * slope)
    weights = jnp.exp2((scores - peak) * slope)
    peak_ref[...] = peak
    sum_ref[...] = sum_ref[...] * shrink + jnp.sum(weights, axis=1, keepdims=True)
    mixed_ref[...] = mixed_ref[...] * shrink + jnp.dot(
        weights.astype(jnp.bfloat16), values, preferred_element_type=jnp.float32
    )

    local = token_ref[...] - step * count
    lanes = lax.broadcasted_iota(jnp.int32, (token_ref.shape[0], count), 1)
    choose = jnp.where(lanes == local, 1.0, 0.0).astype(jnp.bfloat16)
    page_key_ref[...] += jnp.dot(choose, keys, preferred_element_type=jnp.float32)
    page_value_ref[...] += jnp.dot(choose, values, preferred_element_type=jnp.float32)

    @pl.when(step == pl.num_programs(0) - 1)
    def _():
        mixed_ref[...] = mixed_ref[...] / sum_ref[...]
        for head in range(GROUP):
            attended_ref[:, head * head_dim : (head + 1) * head_dim] = mixed_ref[
                pl.ds(head, attended_ref.shape[0], stride=GROUP), :
            ].astype(jnp.bfloat16)
        for token in range(PAGE):
            for at, held in enumerate((page_key_ref, page_value_ref)):
                start = (2 * token + at) * head_dim
                pages_ref[:, start : start + head_dim] = held[
                    pl.ds(token, pages_ref.shape[0], stride=PAGE), :
                ].astype(jnp.bfloat16)


def blend(everything, turn, key_pos, queries, query_pos, tokens):
    count, unit, width = everything.shape
    head_dim = width // 2
    together = 4
    steps = count // together
    query_count = queries.shape[0]
    token_count = tokens.shape[0]

    def whole(shape):
        return pl.BlockSpec(shape, lambda i: (0, 0))

    return pl.pallas_call(
        blend_kernel,
        grid=(steps,),
        out_shape=(
            jax.ShapeDtypeStruct((query_count // GROUP, GROUP * head_dim), jnp.bfloat16),
            jax.ShapeDtypeStruct((token_count // PAGE, PAGE * width), jnp.bfloat16),
        ),
        in_specs=[
            pl.BlockSpec((together, unit, width), lambda i: (i, 0, 0)),
            pl.BlockSpec((together, token_count // PAGE, head_dim), lambda i: (i, 0, 0)),
            pl.BlockSpec((1, 1, together * unit), lambda i: (i, 0, 0)),
            whole((query_count, head_dim)),
            whole((query_count, 1)),
            whole((token_count, 1)),
        ],
        out_specs=(
            whole((query_count // GROUP, GROUP * head_dim)),
            whole((token_count // PAGE, PAGE * width)),
        ),
        scratch_shapes=[
            pltpu.VMEM((query_count, 1), jnp.float32),
            pltpu.VMEM((query_count, 1), jnp.float32),
            pltpu.VMEM((query_count, head_dim), jnp.float32),
            pltpu.VMEM((token_count, head_dim), jnp.float32),
            pltpu.VMEM((token_count, head_dim), jnp.float32),
        ],
    )(
        everything,
        turn,
        key_pos.reshape(steps, 1, together * unit),
        queries,
        query_pos[:, None],
        tokens[:, None],
    )


def pick(one_hot, table):
    return jnp.dot(one_hot.astype(jnp.float32), table, precision=lax.Precision.HIGHEST)


def shards(
    pool_kv, pool_slot, passage_order, passage_start, recompute_pos, page_table, fresh_q, fresh_kv
):
    seq_count = lax.axis_size("seq")
    my_index = lax.axis_index("seq")
    page_count = pool_kv.shape[0]
    head_dim = fresh_kv.shape[1] // 2
    half_dim = head_dim // 2
    sel_count = fresh_q.shape[0]
    tok_count = page_count * PAGE
    total_pages = seq_count * page_count
    bf16 = jnp.bfloat16

    filled = tok_count + sel_count
    unit = -(-filled // 64) * 64
    far = jnp.int32(2**30)

    passage_ids = jnp.arange(seq_count, dtype=jnp.int32)
    mine = (passage_ids == my_index)[:, None]
    picked = jnp.sum(jnp.where(mine, recompute_pos, 0), axis=0)
    start_pos = jnp.sum(jnp.where(mine[:, 0], passage_start, 0))
    fresh_pos = start_pos + picked
    fresh_keys = rotate_pos(fresh_kv[:, :head_dim].astype(jnp.float32), fresh_pos).astype(bf16)
    block = jnp.concatenate(
        [
            pool_kv.reshape(tok_count, 2 * head_dim),
            jnp.concatenate([fresh_keys, fresh_kv[:, head_dim:]], axis=1),
            jnp.zeros((unit - filled, 2 * head_dim), bf16),
        ],
        axis=0,
    )
    everything = spread(block, seq_count)

    placed = passage_order[:, None] == passage_ids[None, :]
    slots = jnp.sum(jnp.where(placed, pool_slot[None, :], 0), axis=1)

    frequency = ROPE_BASE ** (-(jnp.arange(half_dim, dtype=jnp.float32) * (2.0 / head_dim)))
    start_angles = passage_start.astype(jnp.float32)[:, None] * frequency
    start_table = jnp.concatenate([jnp.cos(start_angles), jnp.sin(start_angles)], axis=1)
    recompute_rows = recompute_pos.astype(jnp.float32)

    row_ids = jnp.arange(total_pages, dtype=jnp.int32)
    spot = (row_ids % page_count) * seq_count + row_ids // page_count
    row_slot = spot // page_count
    row_page = spot % page_count
    row_hot = row_slot[:, None] == slots[None, :]
    row_passage = jnp.sum(jnp.where(row_hot, passage_ids[None, :], 0), axis=1)
    row_turn = pick(row_hot, start_table)
    row_recompute = pick(row_hot, recompute_rows)
    lane = jnp.arange(PAGE, dtype=jnp.int32)
    row_tok = row_page[:, None] * PAGE + lane[None, :]
    replaced = jnp.any(
        row_recompute[:, None, :] == row_tok[:, :, None].astype(jnp.float32), axis=2
    )
    cached_pos = jnp.where(replaced, far, row_passage[:, None] * tok_count + row_tok).reshape(-1)
    fresh_place = passage_ids[:, None] * tok_count + recompute_pos
    key_pos = jnp.concatenate(
        [
            cached_pos.reshape(seq_count, tok_count),
            fresh_place,
            jnp.full((seq_count, unit - filled), far, jnp.int32),
        ],
        axis=1,
    )
    turn = row_turn.reshape(seq_count, page_count, head_dim)

    my_rows = my_index * page_count + jnp.arange(page_count, dtype=jnp.int32)
    source = jnp.sum(
        jnp.where(
            page_table[None, :] == my_rows[:, None],
            jnp.arange(total_pages, dtype=jnp.int32)[None, :],
            0,
        ),
        axis=1,
    )
    source_passage = source // page_count
    source_page = source % page_count
    source_hot = source_passage[:, None] == passage_ids[None, :]
    source_spot = (
        jnp.sum(jnp.where(source_hot, slots[None, :], 0), axis=1) * page_count + source_page
    )
    source_row = (source_spot % seq_count) * unit + source_spot // seq_count * PAGE
    source_recompute = pick(source_hot, recompute_rows)
    source_tok = source_page[:, None] * PAGE + lane[None, :]
    match = source_recompute[:, None, :] == source_tok[:, :, None].astype(jnp.float32)
    sel_ids = jnp.arange(sel_count, dtype=jnp.int32)
    sel_at = jnp.sum(jnp.where(match, sel_ids[None, None, :] + 1, 0), axis=2)
    token_at = jnp.where(
        sel_at > 0,
        source_passage[:, None] * unit + tok_count + sel_at - 1,
        source_row[:, None] + lane[None, :],
    ).reshape(-1)
    queries = rotate_pos(
        fresh_q.reshape(sel_count, GROUP, head_dim).astype(jnp.float32), fresh_pos[:, None]
    ).astype(bf16)
    query_rows = queries.reshape(-1, head_dim)
    query_pos = jnp.repeat(my_index * tok_count + picked, GROUP)
    attended, pages = blend(everything, turn, key_pos, query_rows, query_pos, token_at)
    return (attended, pages)


def solution(mesh):
    placed = (
        P(("groups", "seq"), None),
        P("groups"),
        P("groups"),
        P("groups"),
        P("groups", None),
        P("groups"),
        P(("groups", "seq"), None),
        P(("groups", "seq"), None),
    )
    return jax.shard_map(
        shards,
        mesh=mesh,
        in_specs=placed,
        out_specs=(P(("groups", "seq"), None), P(("groups", "seq"), None)),
        check_vma=False,
    )
```

```python
import jax
import jax.numpy as jnp
from jax import lax
from jax.experimental import pallas as pl
from jax.experimental.pallas import tpu as pltpu
from jax.sharding import PartitionSpec as P

GROUP = 8
PAGE = 4


ROPE_BASE = 500000.0
LOG2_E = 1.4426950408889634


def rotate_pos(vector, positions):
    half_dim = vector.shape[-1] // 2
    frequency = ROPE_BASE ** (-(jnp.arange(half_dim, dtype=jnp.float32) * (2.0 / vector.shape[-1])))
    angles = positions.astype(jnp.float32)[..., None] * frequency
    cosine = jnp.cos(angles)
    sine = jnp.sin(angles)
    lower_half = vector[..., :half_dim]
    upper_half = vector[..., half_dim:]
    return jnp.concatenate(
        [lower_half * cosine - upper_half * sine, upper_half * cosine + lower_half * sine], axis=-1
    )


MESH = pl.DeviceIdType.MESH


PIECES = 3


def piece_rows(rows, count):
    halves = max(2, 2 * (count // 4 - 1))
    cut = rows * (halves - 1) // halves // 16 * 16
    size = -(-cut // (PIECES * 16)) * 16
    return [(at, min(size, cut - at)) for at in range(0, cut, size)] + [(cut, rows - cut)]


def spread_kernel(count, block_ref, all_ref, send_sem, recv_sem, own_sem):
    rows = block_ref.shape[0]
    length = count // 4
    parts = [pl.ds(*piece) for piece in piece_rows(rows, count)]
    last = len(parts) - 1
    lined = range(last)
    me = lax.axis_index("seq")
    at = me // 4
    inner = lax.rem(me, 4)
    core = lax.rem(inner, 2)
    across_inner = lax.rem(inner + 2, 4)
    across = at * 4 + across_inner
    sibling = me + 1 - 2 * core
    twin_inner = inner + 1 - 2 * core
    up, down = me + 4, me - 4
    has_up, has_down = at < length - 1, at > 0

    barrier = pltpu.get_barrier_semaphore()

    def greet(device):
        pl.semaphore_signal(barrier, inc=1, device_id={"seq": device}, device_id_type=MESH)

    greet(across)
    greet(sibling)
    pl.when(has_up)(lambda: greet(up))
    pl.when(has_down)(lambda: greet(down))
    pl.semaphore_wait(barrier, 2 + jnp.where(has_up, 1, 0) + jnp.where(has_down, 1, 0))

    def copy(part, block, way, device, own=False):
        source = block_ref.at[parts[part]] if own else all_ref.at[block, parts[part]]
        return pltpu.make_async_remote_copy(
            src_ref=source,
            dst_ref=all_ref.at[block, parts[part]],
            send_sem=send_sem.at[way, part, block],
            recv_sem=recv_sem.at[part, block],
            device_id={"seq": device},
            device_id_type=MESH,
        )

    def begin(part, block, way, device, own=False):
        copy(part, block, way, device, own).start()

    def arrive(part, block):
        copy(part, block, 0, sibling).wait_recv()

    local = pltpu.make_async_copy(block_ref, all_ref.at[me], own_sem)
    local.start()

    def send_own(act):
        act(last, me, 2, across, True)
        for part in lined:
            pl.when(has_up)(lambda part=part: act(part, me, 0, up, True))
            pl.when(has_down)(lambda part=part: act(part, me, 1, down, True))
        pl.when(has_up)(lambda: act(last, me, 0, up, True))
        pl.when(has_down)(lambda: act(last, me, 1, down, True))
        for part in lined:
            act(part, me, 2, across, True)
        for part in (last, *lined):
            act(part, me, 3, sibling, True)

    def pass_across_first(act):
        pl.when(has_up)(lambda: act(last, across, 0, up))
        pl.when(has_down)(lambda: act(last, across, 1, down))
        act(last, across, 3, sibling)

    def each(step, act, wait):
        for part, where, cross in (
            *((part, inner, True) for part in lined),
            (last, inner, False),
            (last, across_inner, False),
        ):
            for way, exists, more, device, place in (
                (0, at - step >= 0, has_up, up, at - step),
                (1, at + step < length, has_down, down, at + step),
            ):
                block = place * 4 + where

                @pl.when(exists)
                def _(part=part, block=block, cross=cross, way=way, more=more, device=device):
                    if wait:
                        arrive(part, block)
                    pl.when(more)(lambda: act(part, block, way, device))
                    if cross:
                        act(part, block, 2, across)
                    act(part, block, 3, sibling)

    def crossed(step, act, wait):
        for exists, place in ((at - step >= 0, at - step), (at + step < length, at + step)):

            @pl.when(exists)
            def _(place=place):
                block = place * 4 + across_inner
                for part in lined:
                    if wait:
                        arrive(part, block)
                    act(part, block, 3, sibling)

    def crossed_here(act, wait):
        for part in lined:
            if wait:
                arrive(part, across)
            act(part, across, 3, sibling)

    send_own(begin)
    arrive(last, across)
    pass_across_first(begin)

    @pl.loop(1, length)
    def _(step):
        each(step, begin, True)
        pl.when(step == 1)(lambda: crossed_here(begin, True))
        pl.when(step > 1)(lambda: crossed(step - 1, begin, True))

    if length == 1:
        crossed_here(begin, True)
    else:
        crossed(length - 1, begin, True)

    @pl.loop(0, length)
    def _(place):
        for other in range(2):
            block = place * 4 + other * 2 + lax.rem(core + 1, 2)
            for part in range(last + 1):
                arrive(part, block)

    def settle(part, block, way, device, own=False):
        copy(part, block, way, device, own).wait_send()

    send_own(settle)
    pass_across_first(settle)

    @pl.loop(1, length)
    def _(step):
        each(step, settle, False)
        crossed(step, settle, False)

    crossed_here(settle, False)
    local.wait()


def spread(block, count):
    rows, width = block.shape
    return pl.pallas_call(
        lambda *refs: spread_kernel(count, *refs),
        out_shape=jax.ShapeDtypeStruct((count, rows, width), block.dtype),
        in_specs=[pl.BlockSpec(memory_space=pltpu.VMEM)],
        out_specs=pl.BlockSpec(memory_space=pl.ANY),
        scratch_shapes=[
            pltpu.SemaphoreType.DMA((4, len(piece_rows(rows, count)), count)),
            pltpu.SemaphoreType.DMA((len(piece_rows(rows, count)), count)),
            pltpu.SemaphoreType.DMA,
        ],
        compiler_params=pltpu.CompilerParams(collective_id=0, has_side_effects=True),
    )(block)


def blend_kernel(
    all_ref, turn_ref, key_pos_ref, query_ref, query_pos_ref, token_ref,
    attended_ref, pages_ref, peak_ref, sum_ref, mixed_ref, page_key_ref, page_value_ref,
):
    step = pl.program_id(0)
    together, unit, width = all_ref.shape
    head_dim = width // 2
    half_dim = head_dim // 2
    count = together * unit

    @pl.when(step == 0)
    def _():
        peak_ref[...] = jnp.full(peak_ref.shape, -1e30, jnp.float32)
        sum_ref[...] = jnp.zeros(sum_ref.shape, jnp.float32)
        mixed_ref[...] = jnp.zeros(mixed_ref.shape, jnp.float32)
        page_key_ref[...] = jnp.zeros(page_key_ref.shape, jnp.float32)
        page_value_ref[...] = jnp.zeros(page_value_ref.shape, jnp.float32)

    rows = all_ref[...].reshape(count, width)
    raw = rows[:, :head_dim].astype(jnp.float32)
    values = rows[:, head_dim:]
    pages = turn_ref.shape[1]
    owner = lax.broadcasted_iota(jnp.int32, (unit, pages), 0) // PAGE
    expand = jnp.where(
        owner == lax.broadcasted_iota(jnp.int32, (unit, pages), 1), 1.0, 0.0
    ).astype(jnp.bfloat16)

    def unfold(table):
        high = table.astype(jnp.bfloat16)
        rest = table - high.astype(jnp.float32)
        middle = rest.astype(jnp.bfloat16)
        low = (rest - middle.astype(jnp.float32)).astype(jnp.bfloat16)
        thirds = jnp.dot(
            expand,
            jnp.concatenate([high, middle, low], axis=1),
            preferred_element_type=jnp.float32,
        )
        return (
            thirds[:, :head_dim]
            + thirds[:, head_dim : 2 * head_dim]
            + thirds[:, 2 * head_dim :]
        )

    at_row = lax.broadcasted_iota(jnp.int32, (unit, head_dim), 0)
    at_lane = lax.broadcasted_iota(jnp.int32, (unit, head_dim), 1)
    still = jnp.where((at_row >= pages * PAGE) & (at_lane < half_dim), 1.0, 0.0)
    turn = jnp.concatenate(
        [
            unfold(turn_ref[part])
            + still
            for part in range(together)
        ],
        axis=0,
    )
    turned = pltpu.roll(turn, half_dim, 1)
    first = lax.broadcasted_iota(jnp.int32, (count, head_dim), 1) < half_dim
    cosine = jnp.where(first, turn, turned)
    sine = jnp.where(first, -turned, turn)
    keys = (raw * cosine + pltpu.roll(raw, half_dim, 1) * sine).astype(jnp.bfloat16)

    scores = lax.dot_general(
        query_ref[...], keys, (((1,), (1,)), ((), ())), preferred_element_type=jnp.float32
    )
    slope = head_dim ** (-0.5) * LOG2_E
    scores = jnp.where(key_pos_ref[0] <= query_pos_ref[...], scores, -1e30)
    old_peak = peak_ref[...]
    peak = jnp.maximum(old_peak, jnp.max(scores, axis=1, keepdims=True))
    shrink = jnp.exp2((old_peak - peak) * slope)
    weights = jnp.exp2((scores - peak) * slope)
    peak_ref[...] = peak
    sum_ref[...] = sum_ref[...] * shrink + jnp.sum(weights, axis=1, keepdims=True)
    mixed_ref[...] = mixed_ref[...] * shrink + jnp.dot(
        weights.astype(jnp.bfloat16), values, preferred_element_type=jnp.float32
    )

    local = token_ref[...] - step * count
    lanes = lax.broadcasted_iota(jnp.int32, (token_ref.shape[0], count), 1)
    choose = jnp.where(lanes == local, 1.0, 0.0).astype(jnp.bfloat16)
    page_key_ref[...] += jnp.dot(choose, keys, preferred_element_type=jnp.float32)
    page_value_ref[...] += jnp.dot(choose, values, preferred_element_type=jnp.float32)

    @pl.when(step == pl.num_programs(0) - 1)
    def _():
        mixed_ref[...] = mixed_ref[...] / sum_ref[...]
        for head in range(GROUP):
            attended_ref[:, head * head_dim : (head + 1) * head_dim] = mixed_ref[
                pl.ds(head, attended_ref.shape[0], stride=GROUP), :
            ].astype(jnp.bfloat16)
        for token in range(PAGE):
            for at, held in enumerate((page_key_ref, page_value_ref)):
                start = (2 * token + at) * head_dim
                pages_ref[:, start : start + head_dim] = held[
                    pl.ds(token, pages_ref.shape[0], stride=PAGE), :
                ].astype(jnp.bfloat16)


def blend(everything, turn, key_pos, queries, query_pos, tokens):
    count, unit, width = everything.shape
    head_dim = width // 2
    together = 4
    steps = count // together
    query_count = queries.shape[0]
    token_count = tokens.shape[0]

    def whole(shape):
        return pl.BlockSpec(shape, lambda i: (0, 0))

    return pl.pallas_call(
        blend_kernel,
        grid=(steps,),
        out_shape=(
            jax.ShapeDtypeStruct((query_count // GROUP, GROUP * head_dim), jnp.bfloat16),
            jax.ShapeDtypeStruct((token_count // PAGE, PAGE * width), jnp.bfloat16),
        ),
        in_specs=[
            pl.BlockSpec((together, unit, width), lambda i: (i, 0, 0)),
            pl.BlockSpec((together, token_count // PAGE, head_dim), lambda i: (i, 0, 0)),
            pl.BlockSpec((1, 1, together * unit), lambda i: (i, 0, 0)),
            whole((query_count, head_dim)),
            whole((query_count, 1)),
            whole((token_count, 1)),
        ],
        out_specs=(
            whole((query_count // GROUP, GROUP * head_dim)),
            whole((token_count // PAGE, PAGE * width)),
        ),
        scratch_shapes=[
            pltpu.VMEM((query_count, 1), jnp.float32),
            pltpu.VMEM((query_count, 1), jnp.float32),
            pltpu.VMEM((query_count, head_dim), jnp.float32),
            pltpu.VMEM((token_count, head_dim), jnp.float32),
            pltpu.VMEM((token_count, head_dim), jnp.float32),
        ],
    )(
        everything,
        turn,
        key_pos.reshape(steps, 1, together * unit),
        queries,
        query_pos[:, None],
        tokens[:, None],
    )


def pick(one_hot, table):
    return jnp.dot(one_hot.astype(jnp.float32), table, precision=lax.Precision.HIGHEST)


def shards(
    pool_kv, pool_slot, passage_order, passage_start, recompute_pos, page_table, fresh_q, fresh_kv
):
    seq_count = lax.axis_size("seq")
    my_index = lax.axis_index("seq")
    page_count = pool_kv.shape[0]
    head_dim = fresh_kv.shape[1] // 2
    half_dim = head_dim // 2
    sel_count = fresh_q.shape[0]
    tok_count = page_count * PAGE
    total_pages = seq_count * page_count
    bf16 = jnp.bfloat16

    filled = tok_count + sel_count
    unit = -(-filled // 64) * 64
    far = jnp.int32(2**30)

    passage_ids = jnp.arange(seq_count, dtype=jnp.int32)
    mine = (passage_ids == my_index)[:, None]
    picked = jnp.sum(jnp.where(mine, recompute_pos, 0), axis=0)
    start_pos = jnp.sum(jnp.where(mine[:, 0], passage_start, 0))
    fresh_pos = start_pos + picked
    fresh_keys = rotate_pos(fresh_kv[:, :head_dim].astype(jnp.float32), fresh_pos).astype(bf16)
    block = jnp.concatenate(
        [
            pool_kv.reshape(tok_count, 2 * head_dim),
            jnp.concatenate([fresh_keys, fresh_kv[:, head_dim:]], axis=1),
            jnp.zeros((unit - filled, 2 * head_dim), bf16),
        ],
        axis=0,
    )
    everything = spread(block, seq_count)

    placed = passage_order[:, None] == passage_ids[None, :]
    slots = jnp.sum(jnp.where(placed, pool_slot[None, :], 0), axis=1)

    frequency = ROPE_BASE ** (-(jnp.arange(half_dim, dtype=jnp.float32) * (2.0 / head_dim)))
    start_angles = passage_start.astype(jnp.float32)[:, None] * frequency
    start_table = jnp.concatenate([jnp.cos(start_angles), jnp.sin(start_angles)], axis=1)
    recompute_rows = recompute_pos.astype(jnp.float32)

    row_ids = jnp.arange(total_pages, dtype=jnp.int32)
    spot = (row_ids % page_count) * seq_count + row_ids // page_count
    row_slot = spot // page_count
    row_page = spot % page_count
    row_hot = row_slot[:, None] == slots[None, :]
    row_passage = jnp.sum(jnp.where(row_hot, passage_ids[None, :], 0), axis=1)
    row_turn = pick(row_hot, start_table)
    row_recompute = pick(row_hot, recompute_rows)
    lane = jnp.arange(PAGE, dtype=jnp.int32)
    row_tok = row_page[:, None] * PAGE + lane[None, :]
    replaced = jnp.any(
        row_recompute[:, None, :] == row_tok[:, :, None].astype(jnp.float32), axis=2
    )
    cached_pos = jnp.where(replaced, far, row_passage[:, None] * tok_count + row_tok).reshape(-1)
    fresh_place = passage_ids[:, None] * tok_count + recompute_pos
    key_pos = jnp.concatenate(
        [
            cached_pos.reshape(seq_count, tok_count),
            fresh_place,
            jnp.full((seq_count, unit - filled), far, jnp.int32),
        ],
        axis=1,
    )
    turn = row_turn.reshape(seq_count, page_count, head_dim)

    my_rows = my_index * page_count + jnp.arange(page_count, dtype=jnp.int32)
    source = jnp.sum(
        jnp.where(
            page_table[None, :] == my_rows[:, None],
            jnp.arange(total_pages, dtype=jnp.int32)[None, :],
            0,
        ),
        axis=1,
    )
    source_passage = source // page_count
    source_page = source % page_count
    source_hot = source_passage[:, None] == passage_ids[None, :]
    source_spot = (
        jnp.sum(jnp.where(source_hot, slots[None, :], 0), axis=1) * page_count + source_page
    )
    source_row = (source_spot % seq_count) * unit + source_spot // seq_count * PAGE
    source_recompute = pick(source_hot, recompute_rows)
    source_tok = source_page[:, None] * PAGE + lane[None, :]
    match = source_recompute[:, None, :] == source_tok[:, :, None].astype(jnp.float32)
    sel_ids = jnp.arange(sel_count, dtype=jnp.int32)
    sel_at = jnp.sum(jnp.where(match, sel_ids[None, None, :] + 1, 0), axis=2)
    token_at = jnp.where(
        sel_at > 0,
        source_passage[:, None] * unit + tok_count + sel_at - 1,
        source_row[:, None] + lane[None, :],
    ).reshape(-1)
    queries = rotate_pos(
        fresh_q.reshape(sel_count, GROUP, head_dim).astype(jnp.float32), fresh_pos[:, None]
    ).astype(bf16)
    query_rows = queries.reshape(-1, head_dim)
    query_pos = jnp.repeat(my_index * tok_count + picked, GROUP)
    attended, pages = blend(everything, turn, key_pos, query_rows, query_pos, token_at)
    return (attended, pages)


def solution(mesh):
    placed = (
        P(("groups", "seq"), None),
        P("groups"),
        P("groups"),
        P("groups"),
        P("groups", None),
        P("groups"),
        P(("groups", "seq"), None),
        P(("groups", "seq"), None),
    )
    return jax.shard_map(
        shards,
        mesh=mesh,
        in_specs=placed,
        out_specs=(P(("groups", "seq"), None), P(("groups", "seq"), None)),
        check_vma=False,
    )
```
